256 devices in a mesh: section: 8 (over x, core), seq: 32 (over z, y).
Axes of the slice: x: 4, y: 4, z: 8, core: 2. Of those that a mesh axis runs over, the one named last changes fastest.
Arguments:
- saved_section_input: bfloat16 [8, 4096, 1024], P('section', 'seq'), may hold values from -6 to 6
- out_cot: bfloat16 [8, 4096, 1024], P('section', 'seq'), may hold values from -6 to 6
- kernel_weight: bfloat16 [8, 2, 3, 64, 16, 32], P('section'), may hold values from -0.875 to 0.875
- blend_weight: bfloat16 [8, 2, 1024, 1024], P('section'), may hold values from -0.1875 to 0.1875
- hazard_head: bfloat16 [1024, 64], replicated, may hold values from -0.75 to 0.75
- labels: int32 [4096], P('seq'), may hold values from 0 to 63
- events: int32 [4096], P('seq'), may hold values 0 or 1
Outputs:
- input_grad: bfloat16 [8, 4096, 1024], P('section', 'seq')
- next_cot: bfloat16 [8, 4096, 1024], P('section', 'seq')
- mix_grad: float32 [8, 1024, 2, 1024], P('section', 'seq')
- conv_grad: float32 [8, 2, 3, 64, 16, 32], P('section', None, None, 'seq')
The draws below stay inside these ranges and needn't reach their ends.
All inputs are finite; a program needn't handle non-finite values. No bound on the sum of `events` on one device may be relied on, other than what follows from the above.
Results may differ from the reference program's by a relative error of at most 0.006.
Values may be sent and summed in bfloat16 or wider, within the bound.
A program may use at most 64 MiB of HBM per device.

```python
import jax
import jax.numpy as jnp
from jax import lax

C = 1024
GROUPS = 64
BINS = 64
GSIZE = 16
NARROW_SPACING = 16
WIDE_SPACING = 256
TOKENS = 4096
N_SECTION = 8


def touch_ends(drawn, own_key, least, largest):
    longest = drawn.shape.index(max(drawn.shape))
    spots = []
    for shift in (0, 1):
        where = [jax.random.randint(jax.random.fold_in(own_key, axis), (), 0, length) for axis, length in enumerate(drawn.shape)]
        where[longest] = (where[longest] + shift) % drawn.shape[longest]
        spots.append(tuple(where))
    return drawn.at[spots[0]].set(least).at[spots[1]].set(largest)


def block_scale(rng, extent, split, low, high):
    def one(dim, shards_of):
        heights = jax.random.uniform(jax.random.fold_in(jax.random.fold_in(rng, 6), dim), (shards_of,), jnp.float32, low / len(split), high / len(split))
        return jnp.repeat(jnp.exp(heights), extent[dim] // shards_of).reshape((-1,) + (1,) * (len(extent) - dim - 1))

    factor_of = one(*split[0])
    for cut in split[1:]:
        factor_of = factor_of * one(*cut)
    return factor_of


def normal_values(stream_key, extent, deviation, bound, shards=(), kind=jnp.bfloat16):
    result = deviation * jax.random.normal(stream_key, extent, jnp.float32)
    if shards:
        result = result * block_scale(stream_key, extent, shards, -0.22, 0.18)
    return jnp.clip(result, -bound, bound).astype(kind)


def setup_inputs(seed: int = 0) -> dict:
    seeds = jax.random.split(jax.random.key(seed), 8)
    return {
        "saved_section_input": normal_values(seeds[0], (N_SECTION, TOKENS, C), 1.0, 6.0, ((0, 8), (1, 32))),
        "out_cot": normal_values(seeds[1], (N_SECTION, TOKENS, C), 1.0, 6.0, ((0, 8), (1, 32))),
        "kernel_weight": normal_values(seeds[2], (N_SECTION, 2, 3, GROUPS, GSIZE, 2 * GSIZE), (3 * GSIZE) ** -0.5, 0.875, ((0, 8),)),
        "blend_weight": normal_values(seeds[3], (N_SECTION, 2, C, C), C ** -0.5, 0.1875, ((0, 8),)),
        "hazard_head": normal_values(seeds[4], (C, BINS), BINS ** -0.5, 0.75),
        "labels": touch_ends(jax.random.randint(seeds[5], (TOKENS,), 0, BINS), jax.random.fold_in(seeds[5], 1), 0, BINS - 1).astype(jnp.int32),
        "events": touch_ends((jax.random.randint(seeds[6], (TOKENS,), 0, 4) < 3).astype(jnp.int32), jax.random.fold_in(seeds[6], 1), 0, 1),
    }


exact_mode = lax.Precision.HIGHEST

def delayed(values, offset):
    zeros = jnp.zeros((offset,) + values.shape[1:], values.dtype)
    return jnp.concatenate([zeros, values[:values.shape[0] - offset]], axis=0)

def advanced(values, offset):
    zeros = jnp.zeros((offset,) + values.shape[1:], values.dtype)
    return jnp.concatenate([values[offset:], zeros], axis=0)

def gate_values(preact):
    filt = preact[..., :GSIZE].astype(jnp.float32)
    gate_part = preact[..., GSIZE:].astype(jnp.float32)
    return jnp.tanh(filt) * jax.nn.sigmoid(gate_part)

def gate_grad(preact, dgated):
    filt = jnp.tanh(preact[..., :GSIZE].astype(jnp.float32))
    gate_part = jax.nn.sigmoid(preact[..., GSIZE:].astype(jnp.float32))
    return jnp.concatenate([dgated * gate_part * (1.0 - filt * filt), dgated * filt * gate_part * (1.0 - gate_part)], axis=-1)

def layer_forward_pass(hidden, weights, mix_matrix, reach):
    total = hidden.shape[0]
    tap_list = [hidden, delayed(hidden, reach), delayed(hidden, 2 * reach)]
    summed = jnp.zeros((total, GROUPS, 2 * GSIZE), jnp.float32)
    for k in range(3):
        summed = summed + jnp.einsum('rgi,gio->rgo', tap_list[k].reshape(total, GROUPS, GSIZE).astype(jnp.float32), weights[k].astype(jnp.float32), precision=exact_mode)
    preact = summed.astype(jnp.bfloat16)
    gated = gate_values(preact).reshape(total, C).astype(jnp.bfloat16)
    output = (hidden.astype(jnp.float32) + jnp.dot(gated, mix_matrix, preferred_element_type=jnp.float32)).astype(jnp.bfloat16)
    return (tap_list, preact, gated, output)

def layer_reverse_pass(upstream_gradient, tap_list, preact, gated, weights, mix_matrix, reach):
    total = upstream_gradient.shape[0]
    dgated = jnp.dot(upstream_gradient, mix_matrix.T, preferred_element_type=jnp.float32).reshape(total, GROUPS, GSIZE)
    dpre = gate_grad(preact, dgated)
    mix_part = jnp.dot(gated.T, upstream_gradient, preferred_element_type=jnp.float32)
    conv_part = jnp.stack([jnp.einsum('rgi,rgo->gio', tap.reshape(total, GROUPS, GSIZE).astype(jnp.float32), dpre, precision=exact_mode) for tap in tap_list])
    back_sum = upstream_gradient.astype(jnp.float32)
    for k in range(3):
        moved = jnp.einsum('rgo,gio->rgi', dpre, weights[k].astype(jnp.float32), precision=exact_mode).reshape(total, C)
        if k > 0:
            moved = advanced(moved, k * reach)
        back_sum = back_sum + moved
    return (back_sum.astype(jnp.bfloat16), mix_part, conv_part)

def reference(saved_section_input, out_cot, kernel_weight, blend_weight, hazard_head, labels, events):
    input_list = []
    mix_list = []
    conv_list = []
    cot_list = []
    for section_number in range(N_SECTION):
        opening_layer = layer_forward_pass(saved_section_input[section_number], kernel_weight[section_number, 0], blend_weight[section_number, 0], NARROW_SPACING)
        closing_layer = layer_forward_pass(opening_layer[3], kernel_weight[section_number, 1], blend_weight[section_number, 1], WIDE_SPACING)
        if section_number == N_SECTION - 1:
            logits = jnp.dot(closing_layer[3], hazard_head, preferred_element_type=jnp.float32)
            hazard = jax.nn.sigmoid(logits)
            bin_ids = jnp.arange(BINS, dtype=jnp.int32)[None, :]
            below = (bin_ids <= labels[:, None]).astype(jnp.float32)
            at_label = (bin_ids == labels[:, None]).astype(jnp.float32) * events[:, None].astype(jnp.float32)
            dlogit = (hazard * below - at_label).astype(jnp.bfloat16)
            loss_cot = jnp.dot(dlogit, hazard_head.T, preferred_element_type=jnp.float32)
            upstream_gradient = (out_cot[section_number].astype(jnp.float32) + loss_cot).astype(jnp.bfloat16)
        else:
            upstream_gradient = out_cot[section_number]
        cot_list.append(upstream_gradient)
        between_gradient, blend_wide, convolution_wide = layer_reverse_pass(upstream_gradient, closing_layer[0], closing_layer[1], closing_layer[2], kernel_weight[section_number, 1], blend_weight[section_number, 1], WIDE_SPACING)
        input_gradient_rows, blend_narrow, convolution_narrow = layer_reverse_pass(between_gradient, opening_layer[0], opening_layer[1], opening_layer[2], kernel_weight[section_number, 0], blend_weight[section_number, 0], NARROW_SPACING)
        input_list.append(input_gradient_rows)
        mix_list.append(jnp.stack([blend_narrow, blend_wide], axis=1))
        conv_list.append(jnp.stack([convolution_narrow, convolution_wide]))
    next_list = input_list[1:] + [cot_list[-1]]
    return (jnp.stack(input_list), jnp.stack(next_list), jnp.stack(mix_list), jnp.stack(conv_list))
```

```python
import functools

import jax
import jax.numpy as jnp
from jax import lax
from jax.experimental import pallas as pl
from jax.experimental.pallas import tpu as pltpu
from jax.sharding import PartitionSpec as P

MESH = pl.DeviceIdType.MESH
F32 = jnp.float32
BF = jnp.bfloat16
NY = 4
LANE = 128

NT = (((1,), (1,)), ((), ()))
TN = (((0,), (0,)), ((), ()))
NN = (((1,), (0,)), ((), ()))


def mm(a, b, dims):
    return lax.dot_general(a, b, dims, preferred_element_type=F32)


def iota(shape, dim):
    return lax.broadcasted_iota(jnp.int32, shape, dim)


def out_channel(col):
    return jnp.where(col < LANE, col & 15, 16 + (col & 15))


def expand_weights(kw, layer, wbd, groups):
    half = groups * 16 // 2
    sel = jnp.where(
        out_channel(iota((512, 256), 1)) == (iota((512, 256), 0) & 31), 1.0, 0.0
    ).astype(BF)
    keep_in = (iota((half, 512), 1) >> 5) == (iota((half, 512), 0) & 15)
    keep_group = ((iota((half, 256), 0) >> 4) & 7) == ((iota((half, 256), 1) & 127) >> 4)
    for part in range(2):
        pick = jnp.where(
            (iota((half, groups), 0) >> 4) + part * (groups // 2) == iota((half, groups), 1),
            1.0,
            0.0,
        ).astype(BF)
        for k in range(3):
            rows = mm(pick, kw[3 * layer + k], NT)
            rows = jnp.where(keep_in, rows, 0.0).astype(BF)
            full = jnp.where(keep_group, mm(rows, sel, NN), 0.0).astype(BF)
            for b in range(half // LANE):
                wbd[part * (half // LANE) + b, k * LANE : (k + 1) * LANE, :] = full[
                    b * LANE : (b + 1) * LANE
                ]


def kernel(nz, nsec, *refs):
    (x_in, cot_in, kw_in, mix_in, head_in, lab_in, ev_in) = refs[:7]
    (ig_out, nc_out, mg_out, cg_out) = refs[7:11]
    (ext, g, kw, mix, head, lab, ev, wbd, gated, fac, mid, near, far, dpre, acc, snd_n, snd_f,
     rcv_n, rcv_f, btw, tap1, tap2, hal_s, hal_r, nxt, part, fin, lsem, ssem, rsem) = refs[11:41]
    pools = refs[41:]

    rows, chans = mid.shape
    nq = NY * nz
    rd = chans // nq
    blocks = chans // LANE
    groups = chans // 16
    width = part.shape[-1]
    sec = lax.axis_index("section")
    q = lax.axis_index("seq")
    y = lax.rem(q, NY)
    z = q // NY
    last = sec == nsec - 1

    def seq(step):
        return {"seq": lax.rem(q + step + nq, nq)}

    def ydev(step):
        return {"seq": z * NY + lax.rem(y + step + NY, NY)}

    def zdev(step):
        return {"seq": lax.rem(z + step + nz, nz) * NY + y}

    loads = []
    for i, (src, dst) in enumerate(
        [
            (x_in.at[0], ext.at[pl.ds(32, rows)]),
            (kw_in, kw),
            (mix_in.at[0, 0], mix.at[0]),
            (cot_in.at[0], g),
            (mix_in.at[0, 1], mix.at[1]),
            (head_in, head),
            (lab_in, lab),
            (ev_in, ev),
        ]
    ):
        copy = pltpu.make_async_copy(src, dst, lsem.at[i])
        copy.start()
        loads.append(copy)

    count = [0]

    def push(src, dst, target):
        n = count[0]
        count[0] += 1
        copy = pltpu.make_async_remote_copy(
            src_ref=src,
            dst_ref=dst,
            send_sem=ssem.at[n],
            recv_sem=rsem.at[n],
            device_id=target,
            device_id_type=MESH,
        )
        copy.start()
        return copy

    barrier = pltpu.get_barrier_semaphore()
    greet = [seq(1), seq(-1), seq(2), seq(-2), seq(NY), seq(-NY), ydev(1), ydev(-1)]
    greet.append({"section": lax.rem(sec + 1, nsec)})
    for target in greet:
        pl.semaphore_signal(barrier, inc=1, device_id=target, device_id_type=MESH)
    pl.semaphore_wait(barrier, len(greet))

    sends = []
    halo = push(x_in.at[0, pl.ds(rows - 32, 32)], ext.at[pl.ds(0, 32)], seq(1))
    sends.append(halo)

    loads[1].wait()
    expand_weights(kw, 0, wbd.at[0], groups)
    loads[0].wait()
    loads[2].wait()
    halo.wait_recv()

    @pl.when(q == 0)
    def _():
        ext[0:32] = jnp.zeros((32, chans), BF)

    def lanes(b):
        return slice(b * LANE, (b + 1) * LANE)

    def taps_short(b):
        return jnp.concatenate(
            [ext[32 : 32 + rows, lanes(b)], ext[16 : 16 + rows, lanes(b)], ext[0:rows, lanes(b)]],
            axis=1,
        )

    def taps_long(b):
        return jnp.concatenate([mid[:, lanes(b)], near[:, lanes(b)], far[:, lanes(b)]], axis=1)

    def gates(layer, taps):
        for b in range(blocks):
            pre = mm(taps(b), wbd[layer, b], NN).astype(BF).astype(F32)
            filt = jnp.tanh(pre[:, :LANE])
            gate = jax.nn.sigmoid(pre[:, LANE:])
            gated[layer, :, lanes(b)] = (filt * gate).astype(BF)
            fac[layer, 0, :, lanes(b)] = gate * (1.0 - filt * filt)
            fac[layer, 1, :, lanes(b)] = filt * gate * (1.0 - gate)

    gates(0, taps_short)
    mid[...] = (ext[32 : 32 + rows].astype(F32) + mm(gated[0], mix[0], NN)).astype(BF)
    to_near = push(mid, near, seq(2))
    to_far = push(mid, far, seq(NY))
    sends += [to_near, to_far]

    expand_weights(kw, 1, wbd.at[1], groups)
    for copy in loads[3:]:
        copy.wait()
    to_near.wait_recv()
    to_far.wait_recv()

    @pl.when(q < 2)
    def _():
        near[...] = jnp.zeros((rows, chans), BF)

    @pl.when(q < NY)
    def _():
        far[...] = jnp.zeros((rows, chans), BF)

    gates(1, taps_long)

    @pl.when(last)
    def _():
        top = (mid[...].astype(F32) + mm(gated[1], mix[1], NN)).astype(BF)
        hazard = jax.nn.sigmoid(mm(head[...], top, NT))
        bins = iota(hazard.shape, 0)
        below = jnp.where(bins <= lab[...], hazard, 0.0)
        at_label = jnp.where(bins == lab[...], ev[...].astype(F32), 0.0)
        dlogit = (below - at_label).astype(BF)
        g[...] = (g[...].astype(F32) + mm(dlogit, head[...], TN)).astype(BF)

    def cot_of_pre(layer, upstream):
        dgated = mm(upstream, mix[layer], NT)
        for b in range(blocks):
            both = jnp.concatenate(
                [
                    dgated[:, lanes(b)] * fac[layer, 0, :, lanes(b)],
                    dgated[:, lanes(b)] * fac[layer, 1, :, lanes(b)],
                ],
                axis=1,
            ).astype(BF)
            dpre[layer, :, 256 * b : 256 * (b + 1)] = both

    def back_taps(layer, b):
        return mm(dpre[layer, :, 256 * b : 256 * (b + 1)], wbd[layer, b], NT)

    cot_of_pre(1, g[...])
    for b in range(blocks):
        prods = back_taps(1, b)
        acc[:, lanes(b)] = prods[:, :LANE]
        snd_n[:, lanes(b)] = prods[:, LANE : 2 * LANE].astype(BF)
        snd_f[:, lanes(b)] = prods[:, 2 * LANE :].astype(BF)
    back_near = push(snd_n, rcv_n, seq(-2))
    back_far = push(snd_f, rcv_f, seq(-NY))
    sends += [back_near, back_far]

    compact = jnp.where(
        iota((768, LANE), 1) == 32 * (iota((768, LANE), 0) >> 8) + out_channel(iota((768, LANE), 0) & 255),
        1.0,
        0.0,
    ).astype(BF)
    own_group = (iota((LANE, 256), 0) >> 4) == ((iota((LANE, 256), 1) & 127) >> 4)
    per_z = NY * rd

    def weight_terms(layer, taps, upstream):
        for d in range(nz):
            block = mm(gated[layer, :, d * per_z : (d + 1) * per_z], upstream, TN)
            part[layer, d * NY : (d + 1) * NY, :, 0:chans] = block.reshape(NY, rd, chans)
        for b in range(blocks):
            full = mm(taps(b), dpre[layer, :, 256 * b : 256 * (b + 1)], TN)
            kept = jnp.concatenate(
                [
                    jnp.where(own_group, full[k * LANE : (k + 1) * LANE], 0.0).astype(BF)
                    for k in range(3)
                ],
                axis=1,
            )
            packed = mm(kept, compact, NN)
            n = LANE // rd
            part[layer, b * n : (b + 1) * n, :, chans:width] = packed.reshape(n, rd, LANE)

    weight_terms(1, taps_long, g[...])

    back_near.wait_recv()
    back_far.wait_recv()

    @pl.when(q >= nq - 2)
    def _():
        rcv_n[...] = jnp.zeros((rows, chans), BF)

    @pl.when(q >= nq - NY)
    def _():
        rcv_f[...] = jnp.zeros((rows, chans), BF)

    btw[...] = (
        g[...].astype(F32) + acc[...] + rcv_n[...].astype(F32) + rcv_f[...].astype(F32)
    ).astype(BF)
    cot_of_pre(0, btw[...])
    for b in range(blocks):
        prods = back_taps(0, b)
        acc[:, lanes(b)] = prods[:, :LANE]
        tap1[0:rows, lanes(b)] = prods[:, LANE : 2 * LANE]
        tap2[0:rows, lanes(b)] = prods[:, 2 * LANE :]
    hal_s[0:16] = tap2[0:16].astype(BF)
    hal_s[16:32] = (tap1[0:16] + tap2[16:32]).astype(BF)
    back_halo = push(hal_s, hal_r, seq(-1))
    sends.append(back_halo)
    weight_terms(0, taps_short, btw[...])
    tap1[rows : rows + 16] = jnp.zeros((16, chans), F32)
    tap2[rows : rows + 32] = jnp.zeros((32, chans), F32)
    back_halo.wait_recv()

    @pl.when(q == nq - 1)
    def _():
        hal_r[...] = jnp.zeros((32, chans), BF)

    total = btw[...].astype(F32) + acc[...] + tap1[16 : 16 + rows] + tap2[32 : 32 + rows]
    ig_out[0, 0 : rows - 32] = total[0 : rows - 32].astype(BF)
    ig_out[0, rows - 32 : rows] = (total[rows - 32 :] + hal_r[...].astype(F32)).astype(BF)
    to_prev = push(ig_out.at[0], nxt, {"section": lax.rem(sec + nsec - 1, nsec)})
    sends.append(to_prev)

    def ring(n, pos, dev, own, depth, bufs, done):
        right_s, right_r, left_s, left_r = bufs
        half = depth // 2
        arrived = None
        at = 0
        for t in range(1, n // 2 + 1):
            dist = n // 2 - t + 1
            to_r, to_l = lax.rem(pos + dist, n), lax.rem(pos - dist + n, n)
            size = half if t == 1 else depth
            if arrived is not None:
                was, copies = arrived
                for c in copies:
                    c.wait_recv()
            for d in range(depth):
                if t > 1 or d < half:
                    v = own(to_r, d)
                    if t > 2 or (t == 2 and d < half):
                        v = v + right_r[was + d].astype(F32)
                    right_s[at + d] = v.astype(BF)
                if t > 1 or d >= half:
                    v = own(to_l, d)
                    if t > 2 or (t == 2 and d >= half):
                        v = v + left_r[was + (d - half if t == 2 else d)].astype(F32)
                    left_s[at + (d - half if t == 1 else d)] = v.astype(BF)
            copies = [
                push(right_s.at[pl.ds(at, size)], right_r.at[pl.ds(at, size)], dev(1)),
                push(left_s.at[pl.ds(at, size)], left_r.at[pl.ds(at, size)], dev(-1)),
            ]
            sends.extend(copies)
            arrived = (at, copies)
            at += size
            yield
        was, copies = arrived
        for c in copies:
            c.wait_recv()
        for d in range(depth):
            v = own(pos, d)
            if n > 2:
                v = v + right_r[was + d].astype(F32) + left_r[was + d].astype(F32)
            elif d < half:
                v = v + right_r[was + d].astype(F32)
            else:
                v = v + left_r[was + d - half].astype(F32)
            done(d, v)

    def stream(layer, lo, w, y_first, bufs):
        span = slice(lo, lo + w)
        first, mids, second = bufs[0:4], bufs[4], bufs[5:9]
        h = rd // 2

        def keep(d, v):
            mids[d] = v

        def own2(dest, d):
            return mids[dest, d * h : (d + 1) * h, :]

        def finish(d, v):
            fin[layer, d * h : (d + 1) * h, span] = v

        if y_first:
            yield from ring(NY, y, ydev, lambda e, d: part[layer, d * NY + e, :, span], nz, first, keep)
            yield from ring(nz, z, zdev, own2, 2, second, finish)
        else:
            yield from ring(nz, z, zdev, lambda e, d: part[layer, e * NY + d, :, span], NY, first, keep)
            yield from ring(NY, y, ydev, own2, 2, second, finish)

    live = [
        stream(1, 0, width, True, pools[0:9]),
        stream(0, 0, width, False, pools[9:18]),
    ]
    while live:
        for s in list(live):
            try:
                next(s)
            except StopIteration:
                live.remove(s)

    for layer in range(2):
        mg_out[0, :, layer, :] = fin[layer, :, 0:chans]
        for k in range(3):
            cg_out[0, layer, k] = fin[layer, :, chans + 32 * k : chans + 32 * (k + 1)].reshape(
                rd // 16, 16, 32
            )

    to_prev.wait_recv()

    @pl.when(last)
    def _():
        nc_out[0] = g[...]

    @pl.when(jnp.logical_not(last))
    def _():
        nc_out[0] = nxt[...]

    for copy in sends:
        copy.wait_send()


def ring_pool(n, depth, r, w):
    units = depth // 2 + depth * (n // 2 - 1)
    return [pltpu.VMEM((units, r, w), BF)] * 4


def stream_pool(nz, rd, w, y_first):
    n1, n2 = (NY, nz) if y_first else (nz, NY)
    return ring_pool(n1, n2, rd, w) + [pltpu.VMEM((n2, rd, w), F32)] + ring_pool(n2, 2, rd // 2, w)


def solution(mesh):
    nsec, nq = mesh.shape["section"], mesh.shape["seq"]
    nz = nq // NY

    def body(x, cot, kernel_weight, blend, head, labels, events):
        _, rows, chans = x.shape
        groups, gin, gout = kernel_weight.shape[3:]
        rd = chans // nq
        width = chans + LANE
        blocks = chans // LANE
        kw = jnp.transpose(kernel_weight[0], (0, 1, 3, 4, 2)).reshape(6, gin * gout, groups)
        any_ = pl.BlockSpec(memory_space=pl.ANY)
        vm = pl.BlockSpec(memory_space=pltpu.VMEM)
        act = pltpu.VMEM((rows, chans), BF)
        n_push = 8 + 2 * 2 * (NY // 2 + nz // 2)
        scratch = [
            pltpu.VMEM((rows + 32, chans), BF),
            act,
            pltpu.VMEM((6, gin * gout, groups), BF),
            pltpu.VMEM((2, chans, chans), BF),
            pltpu.VMEM((head.shape[1], chans), BF),
            pltpu.VMEM((1, rows), jnp.int32),
            pltpu.VMEM((1, rows), jnp.int32),
            pltpu.VMEM((2, blocks, 3 * LANE, 2 * LANE), BF),
            pltpu.VMEM((2, rows, chans), BF),
            pltpu.VMEM((2, 2, rows, chans), F32),
            act,
            act,
            act,
            pltpu.VMEM((2, rows, 2 * chans), BF),
            pltpu.VMEM((rows, chans), F32),
            act,
            act,
            act,
            act,
            act,
            pltpu.VMEM((rows + 16, chans), F32),
            pltpu.VMEM((rows + 32, chans), F32),
            pltpu.VMEM((32, chans), BF),
            pltpu.VMEM((32, chans), BF),
            act,
            pltpu.VMEM((2, nq, rd, width), F32),
            pltpu.VMEM((2, rd, width), F32),
            pltpu.SemaphoreType.DMA((8,)),
            pltpu.SemaphoreType.DMA((n_push,)),
            pltpu.SemaphoreType.DMA((n_push,)),
        ]
        scratch += stream_pool(nz, rd, width, True) + stream_pool(nz, rd, width, False)
        return pl.pallas_call(
            functools.partial(kernel, nz, nsec),
            out_shape=(
                jax.ShapeDtypeStruct((1, rows, chans), BF),
                jax.ShapeDtypeStruct((1, rows, chans), BF),
                jax.ShapeDtypeStruct((1, rd, 2, chans), F32),
                jax.ShapeDtypeStruct((1, 2, 3, groups // nq, gin, gout), F32),
            ),
            in_specs=[any_] * 7,
            out_specs=(vm, vm, vm, vm),
            scratch_shapes=scratch,
            compiler_params=pltpu.CompilerParams(
                collective_id=0, has_side_effects=True, vmem_limit_bytes=58 * 1024 * 1024
            ),
        )(x, cot, kw, blend, head.T, labels.reshape(1, rows), events.reshape(1, rows))

    return jax.shard_map(
        body,
        mesh=mesh,
        in_specs=(
            P("section", "seq", None),
            P("section", "seq", None),
            P("section", None, None, None, None, None),
            P("section", None, None, None),
            P(),
            P("seq"),
            P("seq"),
        ),
        out_specs=(
            P("section", "seq", None),
            P("section", "seq", None),
            P("section", "seq", None, None),
            P("section", None, None, "seq", None, None),
        ),
        check_vma=False,
    )
```

```python
import functools

import jax
import jax.numpy as jnp
from jax import lax
from jax.experimental import pallas as pl
from jax.experimental.pallas import tpu as pltpu
from jax.sharding import PartitionSpec as P

MESH = pl.DeviceIdType.MESH
F32 = jnp.float32
BF = jnp.bfloat16
NY = 4
LANE = 128

NT = (((1,), (1,)), ((), ()))
TN = (((0,), (0,)), ((), ()))
NN = (((1,), (0,)), ((), ()))


def mm(a, b, dims):
    return lax.dot_general(a, b, dims, preferred_element_type=F32)


def iota(shape, dim):
    return lax.broadcasted_iota(jnp.int32, shape, dim)


def out_channel(col):
    return jnp.where(col < LANE, col & 15, 16 + (col & 15))


def expand_weights(kw, layer, wbd, groups):
    half = groups * 16 // 2
    sel = jnp.where(
        out_channel(iota((512, 256), 1)) == (iota((512, 256), 0) & 31), 1.0, 0.0
    ).astype(BF)
    keep_in = (iota((half, 512), 1) >> 5) == (iota((half, 512), 0) & 15)
    keep_group = ((iota((half, 256), 0) >> 4) & 7) == ((iota((half, 256), 1) & 127) >> 4)
    for part in range(2):
        pick = jnp.where(
            (iota((half, groups), 0) >> 4) + part * (groups // 2) == iota((half, groups), 1),
            1.0,
            0.0,
        ).astype(BF)
        for k in range(3):
            rows = mm(pick, kw[3 * layer + k], NT)
            rows = jnp.where(keep_in, rows, 0.0).astype(BF)
            full = jnp.where(keep_group, mm(rows, sel, NN), 0.0).astype(BF)
            for b in range(half // LANE):
                wbd[part * (half // LANE) + b, k * LANE : (k + 1) * LANE, :] = full[
                    b * LANE : (b + 1) * LANE
                ]


def kernel(nz, nsec, chunks, *refs):
    (x_in, cot_in, kw_in, mix_in, head_in, lab_in, ev_in) = refs[:7]
    (ig_out, nc_out, mg_out, cg_out) = refs[7:11]
    (ext, cot, kw, mix, head, lab, ev, wbd, gated, fac, mid, dpre, acc, snd_n, snd_f, rcv_n, rcv_f,
     tap1, tap2, hal_s, hal_r, nxt, gath, slc_s, slc_r, dlog, cnv_s, cnv_r, zown,
     lsem, ssem, rsem) = refs[11:43]
    zs0, zr0 = refs[43 : 43 + len(chunks)], refs[43 + len(chunks) : 43 + 2 * len(chunks)]
    ring_bufs = refs[43 + 2 * len(chunks) :]

    _, rows, chans = mid.shape
    nq = NY * nz
    rd = chans // nq
    blocks = chans // LANE
    per = LANE // rd
    groups = chans // 16
    sec = lax.axis_index("section")
    q = lax.axis_index("seq")
    y = lax.rem(q, NY)
    z = q // NY
    last = sec == nsec - 1

    def seq(step):
        return {"seq": lax.rem(q + step + nq, nq)}

    def ydev(step):
        return {"seq": z * NY + lax.rem(y + step, NY)}

    def zdev(step):
        return {"seq": lax.rem(z + step, nz) * NY + y}

    def lanes(b):
        return slice(b * LANE, (b + 1) * LANE)

    g, btw = gath.at[1, 0], gath.at[0, 0]
    own_x = ext.at[pl.ds(32, rows)]

    loads = []
    for i, (src, dst) in enumerate(
        [
            (x_in.at[0], own_x),
            (kw_in, kw),
            (mix_in.at[0, 0], mix.at[0]),
            (cot_in.at[0], cot),
            (mix_in.at[0, 1], mix.at[1]),
            (head_in, head),
            (lab_in, lab),
            (ev_in, ev),
        ]
    ):
        copy = pltpu.make_async_copy(src, dst, lsem.at[i])
        copy.start()
        loads.append(copy)

    sends = []

    def push(src, dst, target):
        n = len(sends)
        copy = pltpu.make_async_remote_copy(
            src_ref=src,
            dst_ref=dst,
            send_sem=ssem.at[n],
            recv_sem=rsem.at[n],
            device_id=target,
            device_id_type=MESH,
        )
        copy.start()
        sends.append(copy)
        return copy

    def got(copies):
        for c in copies:
            c.wait_recv()

    barrier = pltpu.get_barrier_semaphore()
    greet = [seq(-1), seq(-2), seq(1), seq(2)]
    greet += [ydev(j) for j in range(1, NY)] + [zdev(j) for j in range(1, nz)]
    greet.append({"section": lax.rem(sec + 1, nsec)})
    for target in greet:
        pl.semaphore_signal(barrier, inc=1, device_id=target, device_id_type=MESH)
    pl.semaphore_wait(barrier, len(greet))

    def share(src, dst):
        return [push(src(j), dst(j), ydev(j)) for j in range(1, NY)]

    loads[0].wait()
    halo = [push(ext.at[pl.ds(rows, 32)], ext.at[pl.ds(0, 32)], seq(1))]
    loads[3].wait()
    cots = share(lambda j: cot, lambda j: gath.at[1, j])
    g[...] = cot[...]

    loads[1].wait()
    expand_weights(kw, 0, wbd.at[0], groups)
    loads[2].wait()
    got(halo)

    @pl.when(q == 0)
    def _():
        ext[0:32] = jnp.zeros((32, chans), BF)

    def taps_short(b):
        return jnp.concatenate(
            [ext[32 : 32 + rows, lanes(b)], ext[16 : 16 + rows, lanes(b)], ext[0:rows, lanes(b)]],
            axis=1,
        )

    def taps_long(b):
        return jnp.concatenate([mid[i, :, lanes(b)] for i in range(3)], axis=1)

    def gates(layer, taps):
        for b in range(blocks):
            pre = mm(taps(b), wbd[layer, b], NN).astype(BF).astype(F32)
            filt = jnp.tanh(pre[:, :LANE])
            gate = jax.nn.sigmoid(pre[:, LANE:])
            gated[layer, :, lanes(b)] = (filt * gate).astype(BF)
            fac[layer, 0, :, lanes(b)] = gate * (1.0 - filt * filt)
            fac[layer, 1, :, lanes(b)] = filt * gate * (1.0 - gate)

    def turn(layer):
        for b in range(blocks):
            turned = gated[layer, :, lanes(b)].T
            for i in range(per):
                d = b * per + i
                slc_s[layer, d % NY, d // NY] = turned[i * rd : (i + 1) * rd]

    def share_slices(layer):
        slc_r[layer, 0] = slc_s[layer, y]
        return share(
            lambda j: slc_s.at[layer, lax.rem(y + j, NY)], lambda j: slc_r.at[layer, j]
        )

    gates(0, taps_short)
    mid[0] = (ext[32 : 32 + rows].astype(F32) + mm(gated[0], mix[0], NN)).astype(BF)
    forth = [push(mid.at[0], mid.at[2], seq(NY)), push(mid.at[0], mid.at[1], seq(2))]

    expand_weights(kw, 1, wbd.at[1], groups)
    turn(0)
    for copy in loads[4:]:
        copy.wait()
    got(forth)
    slices0 = share_slices(0)

    @pl.when(q < 2)
    def _():
        mid[1] = jnp.zeros((rows, chans), BF)

    @pl.when(q < NY)
    def _():
        mid[2] = jnp.zeros((rows, chans), BF)

    gates(1, taps_long)
    turn(1)
    slices1 = share_slices(1)

    def add_loss(ref, grad):
        ref[...] = (ref[...].astype(F32) + mm(grad, head[...], TN)).astype(BF)

    dlog[0] = jnp.zeros(dlog.shape[1:], BF)

    @pl.when(last)
    def _():
        top = (mid[0].astype(F32) + mm(gated[1], mix[1], NN)).astype(BF)
        hazard = jax.nn.sigmoid(mm(head[...], top, NT))
        bins = iota(hazard.shape, 0)
        below = jnp.where(bins <= lab[...], hazard, 0.0)
        at_label = jnp.where(bins == lab[...], ev[...].astype(F32), 0.0)
        dlog[0] = (below - at_label).astype(BF)
        add_loss(g, dlog[0])

    losses = share(lambda j: dlog.at[0], lambda j: dlog.at[j])

    def cot_of_pre(layer, upstream):
        dgated = mm(upstream, mix[layer], NT)
        for b in range(blocks):
            both = jnp.concatenate(
                [
                    dgated[:, lanes(b)] * fac[layer, 0, :, lanes(b)],
                    dgated[:, lanes(b)] * fac[layer, 1, :, lanes(b)],
                ],
                axis=1,
            ).astype(BF)
            dpre[layer, :, 256 * b : 256 * (b + 1)] = both

    def back_taps(layer, b):
        return mm(dpre[layer, :, 256 * b : 256 * (b + 1)], wbd[layer, b], NT)

    cot_of_pre(1, g[...])
    for b in range(blocks):
        prods = back_taps(1, b)
        acc[:, lanes(b)] = prods[:, :LANE]
        snd_n[:, lanes(b)] = prods[:, LANE : 2 * LANE].astype(BF)
        snd_f[:, lanes(b)] = prods[:, 2 * LANE :].astype(BF)
    back = [push(snd_f, rcv_f, seq(-NY)), push(snd_n, rcv_n, seq(-2))]

    compact = jnp.where(
        iota((768, LANE), 1) == 32 * (iota((768, LANE), 0) >> 8) + out_channel(iota((768, LANE), 0) & 255),
        1.0,
        0.0,
    ).astype(BF)
    own_group = (iota((LANE, 256), 0) >> 4) == ((iota((LANE, 256), 1) & 127) >> 4)

    def conv_terms(layer, taps):
        for b in range(blocks):
            full = mm(taps(b), dpre[layer, :, 256 * b : 256 * (b + 1)], TN)
            kept = jnp.concatenate(
                [
                    jnp.where(own_group, full[k * LANE : (k + 1) * LANE], 0.0).astype(BF)
                    for k in range(3)
                ],
                axis=1,
            )
            packed = mm(kept, compact, NN).astype(BF)
            for i in range(per):
                d = b * per + i
                cnv_s[layer, d % NY, d // NY] = packed[i * rd : (i + 1) * rd]
        return share(
            lambda j: cnv_s.at[layer, lax.rem(y + j, NY)], lambda j: cnv_r.at[layer, j - 1]
        )

    convs1 = conv_terms(1, taps_long)

    def quarter(layer, lo, w):
        left = jnp.concatenate(
            [slc_r[layer, j].reshape(nz * rd, rows) for j in range(NY)], axis=1
        )
        right = gath[layer, :, :, lo : lo + w].reshape(NY * rows, w)
        return mm(left, right, NN).reshape(nz, rd, w)

    def spread(buf, dst):
        return [
            push(buf.at[lax.rem(z + j, nz)], dst.at[j - 1], zdev(j)) for j in range(1, nz)
        ]

    got(slices1)
    got(cots)
    got(losses)

    @pl.when(last)
    def _():
        for j in range(1, NY):
            add_loss(gath.at[1, j], dlog[j])

    def ring(own, done):
        right_s, right_r, left_s, left_r = ring_bufs
        arrived, at = None, 0
        for t in range(1, nz // 2 + 1):
            dist = nz // 2 - t + 1
            to_r, to_l = lax.rem(z + dist, nz), lax.rem(z - dist + nz, nz)
            size = 1 if t == 1 else 2
            if arrived is not None:
                was, copies = arrived
                got(copies)
            for d in range(2):
                if t > 1 or d == 0:
                    v = own(to_r, d)
                    if t > 2 or (t == 2 and d == 0):
                        v = v + right_r[was + d].astype(F32)
                    right_s[at + d] = v.astype(BF)
                if t > 1 or d == 1:
                    v = own(to_l, d)
                    if t > 2 or (t == 2 and d == 1):
                        v = v + left_r[was + (0 if t == 2 else d)].astype(F32)
                    left_s[at + (0 if t == 1 else d)] = v.astype(BF)
            copies = [
                push(right_s.at[pl.ds(at, size)], right_r.at[pl.ds(at, size)], zdev(1)),
                push(left_s.at[pl.ds(at, size)], left_r.at[pl.ds(at, size)], zdev(nz - 1)),
            ]
            arrived = (at, copies)
            at += size
            yield
        was, copies = arrived
        got(copies)
        for d in range(2):
            v = own(z, d)
            if nz > 2:
                v = v + right_r[was + d].astype(F32) + left_r[was + d].astype(F32)
            elif d == 0:
                v = v + right_r[was].astype(F32)
            else:
                v = v + left_r[was].astype(F32)
            done(d, v)
        yield

    half = rd // 2
    for lo in range(0, chans, 256):
        zown[1, :, :, lo : lo + 256] = quarter(1, lo, 256)

    def conv_sum(layer, copies):
        got(copies)
        sums = cnv_s[layer, y].astype(F32)
        for j in range(NY - 1):
            sums = sums + cnv_r[layer, j].astype(F32)
        zown[layer, :, :, chans : chans + LANE] = sums
        return sums

    def put_conv(layer, lo, sums):
        for k in range(3):
            cg_out[0, layer, k, lo // 16 : (lo + sums.shape[0]) // 16] = sums[
                :, 32 * k : 32 * (k + 1)
            ].reshape(sums.shape[0] // 16, 16, 32)

    def finish1(d, v):
        mg_out[0, d * half : (d + 1) * half, 1, :] = v[:, 0:chans]
        put_conv(1, d * half, v[:, chans:])

    conv_sum(1, convs1)
    ring1 = ring(lambda e, d: zown[1, e, d * half : (d + 1) * half, :], finish1)
    next(ring1, None)

    got(back)

    @pl.when(q >= nq - 2)
    def _():
        rcv_n[...] = jnp.zeros((rows, chans), BF)

    @pl.when(q >= nq - NY)
    def _():
        rcv_f[...] = jnp.zeros((rows, chans), BF)

    btw[...] = (
        g[...].astype(F32) + acc[...] + rcv_n[...].astype(F32) + rcv_f[...].astype(F32)
    ).astype(BF)
    shared = [
        share(
            lambda j: gath.at[0, 0, :, pl.ds(lo, w)], lambda j: gath.at[0, j, :, pl.ds(lo, w)]
        )
        for lo, w, _ in chunks
    ]

    next(ring1, None)
    cot_of_pre(0, btw[...])
    for b in range(blocks):
        prods = back_taps(0, b)
        acc[:, lanes(b)] = prods[:, :LANE]
        tap1[0:rows, lanes(b)] = prods[:, LANE : 2 * LANE]
        tap2[0:rows, lanes(b)] = prods[:, 2 * LANE :]
    hal_s[0:16] = tap2[0:16].astype(BF)
    hal_s[16:32] = (tap1[0:16] + tap2[16:32]).astype(BF)
    back_halo = push(hal_s, hal_r, seq(-1))
    convs0 = conv_terms(0, taps_short)
    next(ring1, None)
    tap1[rows : rows + 16] = jnp.zeros((16, chans), F32)
    tap2[rows : rows + 32] = jnp.zeros((32, chans), F32)
    back_halo.wait_recv()

    @pl.when(q == nq - 1)
    def _():
        hal_r[...] = jnp.zeros((32, chans), BF)

    total = btw[...].astype(F32) + acc[...] + tap1[16 : 16 + rows] + tap2[32 : 32 + rows]
    ig_out[0, 0 : rows - 32] = total[0 : rows - 32].astype(BF)
    ig_out[0, rows - 32 : rows] = (total[rows - 32 :] + hal_r[...].astype(F32)).astype(BF)
    to_prev = push(ig_out.at[0], nxt, {"section": lax.rem(sec + nsec - 1, nsec)})

    got(slices0)
    over0 = []
    for c, (lo, w, conv) in enumerate(chunks):
        got(shared[c])
        block = quarter(0, lo, w)
        zown[0, :, :, lo : lo + w] = block
        zs0[c][:, :, 0:w] = block.astype(BF)
        if conv:
            zs0[c][:, :, w : w + LANE] = conv_sum(0, convs0).astype(BF)
        over0.append(spread(zs0[c], zr0[c]))
        if c == 0:
            next(ring1, None)
    for _ in range(nz // 2 - 3):
        next(ring1, None)

    def total_of(own, bufs, lo, w):
        v = own
        for j in range(nz - 1):
            v = v + bufs[j, :, lo : lo + w].astype(F32)
        return v

    to_prev.wait_recv()

    @pl.when(last)
    def _():
        nc_out[0] = g[...]

    @pl.when(jnp.logical_not(last))
    def _():
        nc_out[0] = nxt[...]

    for c, (lo, w, conv) in enumerate(chunks):
        got(over0[c])
        mg_out[0, :, 0, lo : lo + w] = total_of(zown[0, z, :, lo : lo + w], zr0[c], 0, w)
        if conv:
            put_conv(0, 0, total_of(zown[0, z, :, chans : chans + LANE], zr0[c], w, LANE))

    for copy in sends:
        copy.wait_send()


def hand_over(*refs):
    srcs, dsts, bufs, (sem_in, sem_out) = refs[:4], refs[4:8], refs[8:12], refs[12:]
    fetch = [pltpu.make_async_copy(a, b, sem_in.at[i]) for i, (a, b) in enumerate(zip(srcs, bufs))]
    store = [pltpu.make_async_copy(a, b, sem_out.at[i]) for i, (a, b) in enumerate(zip(bufs, dsts))]
    for copy in fetch:
        copy.start()
    for before, after in zip(fetch, store):
        before.wait()
        after.start()
    for copy in store:
        copy.wait()


def solution(mesh):
    nsec, nq = mesh.shape["section"], mesh.shape["seq"]
    nz = nq // NY

    def body(x, cot, kernel_weight, blend, head, labels, events):
        _, rows, chans = x.shape
        groups, gin, gout = kernel_weight.shape[3:]
        rd = chans // nq
        blocks = chans // LANE
        kw = jnp.transpose(kernel_weight[0], (0, 1, 3, 4, 2)).reshape(6, gin * gout, groups)
        any_ = pl.BlockSpec(memory_space=pl.ANY)
        vm = pl.BlockSpec(memory_space=pltpu.VMEM)
        act = pltpu.VMEM((rows, chans), BF)
        step = chans // 4
        chunks = [(i * step, step, i == 3) for i in range(4)]
        wide = [w + (LANE if conv else 0) for _, w, conv in chunks]
        n_push = 1 + 3 + 2 + 6 + 3 + 2 + 6 + nz + 12 + 2 + 4 * (nz - 1)
        bins = head.shape[1]
        scratch = [
            pltpu.VMEM((rows + 32, chans), BF),
            act,
            pltpu.VMEM((6, gin * gout, groups), BF),
            pltpu.VMEM((2, chans, chans), BF),
            pltpu.VMEM((bins, chans), BF),
            pltpu.VMEM((1, rows), jnp.int32),
            pltpu.VMEM((1, rows), jnp.int32),
            pltpu.VMEM((2, blocks, 3 * LANE, 2 * LANE), BF),
            pltpu.VMEM((2, rows, chans), BF),
            pltpu.VMEM((2, 2, rows, chans), F32),
            pltpu.VMEM((3, rows, chans), BF),
            pltpu.VMEM((2, rows, 2 * chans), BF),
            pltpu.VMEM((rows, chans), F32),
            act,
            act,
            act,
            act,
            pltpu.VMEM((rows + 16, chans), F32),
            pltpu.VMEM((rows + 32, chans), F32),
            pltpu.VMEM((32, chans), BF),
            pltpu.VMEM((32, chans), BF),
            act,
            pltpu.VMEM((2, NY, rows, chans), BF),
            pltpu.VMEM((2, NY, nz, rd, rows), BF),
            pltpu.VMEM((2, NY, nz, rd, rows), BF),
            pltpu.VMEM((NY, bins, rows), BF),
            pltpu.VMEM((2, NY, nz, rd, LANE), BF),
            pltpu.VMEM((2, NY - 1, nz, rd, LANE), BF),
            pltpu.VMEM((2, nz, rd, chans + LANE), F32),
            pltpu.SemaphoreType.DMA((8,)),
            pltpu.SemaphoreType.DMA((n_push,)),
            pltpu.SemaphoreType.DMA((n_push,)),
        ]
        scratch += [pltpu.VMEM((nz, rd, w), BF) for w in wide]
        scratch += [pltpu.VMEM((nz - 1, rd, w), BF) for w in wide]
        scratch += [pltpu.VMEM((nz - 1, rd // 2, chans + LANE), BF)] * 4
        shapes = (
            jax.ShapeDtypeStruct((1, rows, chans), BF),
            jax.ShapeDtypeStruct((1, rows, chans), BF),
            jax.ShapeDtypeStruct((1, rd, 2, chans), F32),
            jax.ShapeDtypeStruct((1, 2, 3, groups // nq, gin, gout), F32),
        )
        outs = pl.pallas_call(
            functools.partial(kernel, nz, nsec, chunks),
            out_shape=shapes,
            in_specs=[any_] * 7,
            out_specs=(vm, vm, vm, vm),
            scratch_shapes=scratch,
            compiler_params=pltpu.CompilerParams(
                collective_id=0, has_side_effects=True, vmem_limit_bytes=58 * 1024 * 1024
            ),
        )(x, cot, kw, blend, head.T, labels.reshape(1, rows), events.reshape(1, rows))
        return pl.pallas_call(
            hand_over,
            out_shape=shapes,
            in_specs=[any_] * 4,
            out_specs=(any_,) * 4,
            scratch_shapes=[pltpu.VMEM(o.shape, o.dtype) for o in shapes]
            + [pltpu.SemaphoreType.DMA((4,))] * 2,
        )(*outs)

    return jax.shard_map(
        body,
        mesh=mesh,
        in_specs=(
            P("section", "seq", None),
            P("section", "seq", None),
            P("section", None, None, None, None, None),
            P("section", None, None, None),
            P(),
            P("seq"),
            P("seq"),
        ),
        out_specs=(
            P("section", "seq", None),
            P("section", "seq", None),
            P("section", "seq", None, None),
            P("section", None, None, "seq", None, None),
        ),
        check_vma=False,
    )
```

```python
import functools

import jax
import jax.numpy as jnp
from jax import lax
from jax.experimental import pallas as pl
from jax.experimental.pallas import tpu as pltpu
from jax.sharding import PartitionSpec as P

MESH = pl.DeviceIdType.MESH
F32 = jnp.float32
BF = jnp.bfloat16
NY = 4
LANE = 128

NT = (((1,), (1,)), ((), ()))
TN = (((0,), (0,)), ((), ()))
NN = (((1,), (0,)), ((), ()))


def mm(a, b, dims):
    return lax.dot_general(a, b, dims, preferred_element_type=F32)


def iota(shape, dim):
    return lax.broadcasted_iota(jnp.int32, shape, dim)


def out_channel(col):
    return jnp.where(col < LANE, col & 15, 16 + (col & 15))


def expand_weights(kw, layer, wbd, groups):
    half = groups * 16 // 2
    sel = jnp.where(
        out_channel(iota((512, 256), 1)) == (iota((512, 256), 0) & 31), 1.0, 0.0
    ).astype(BF)
    keep_in = (iota((half, 512), 1) >> 5) == (iota((half, 512), 0) & 15)
    keep_group = ((iota((half, 256), 0) >> 4) & 7) == ((iota((half, 256), 1) & 127) >> 4)
    for part in range(2):
        pick = jnp.where(
            (iota((half, groups), 0) >> 4) + part * (groups // 2) == iota((half, groups), 1),
            1.0,
            0.0,
        ).astype(BF)
        for k in range(3):
            rows = mm(pick, kw[3 * layer + k], NT)
            rows = jnp.where(keep_in, rows, 0.0).astype(BF)
            full = jnp.where(keep_group, mm(rows, sel, NN), 0.0).astype(BF)
            for b in range(half // LANE):
                wbd[part * (half // LANE) + b, k * LANE : (k + 1) * LANE, :] = full[
                    b * LANE : (b + 1) * LANE
                ]


def kernel(nz, nsec, chunks, *refs):
    (x_in, cot_in, kw_in, mix_in, head_in, lab_in, ev_in) = refs[:7]
    (ig_out, nc_out, mg_out, cg_out) = refs[7:11]
    (ext, cot, kw, mix, head, lab, ev, wbd, gated, fac, mid, dpre, acc, snd_n, snd_f, rcv_n, rcv_f,
     tap1, tap2, hal_s, hal_r, nxt, gath, slc_s, slc_r, dlog, cnv_s, cnv_r, zown,
     lsem, ssem, rsem) = refs[11:43]
    zs0, zr0 = refs[43 : 43 + len(chunks)], refs[43 + len(chunks) : 43 + 2 * len(chunks)]
    ring_bufs = refs[43 + 2 * len(chunks) :]

    _, rows, chans = mid.shape
    nq = NY * nz
    rd = chans // nq
    blocks = chans // LANE
    per = LANE // rd
    groups = chans // 16
    sec = lax.axis_index("section")
    q = lax.axis_index("seq")
    y = lax.rem(q, NY)
    z = q // NY
    last = sec == nsec - 1

    def seq(step):
        return {"seq": lax.rem(q + step + nq, nq)}

    def ydev(step):
        return {"seq": z * NY + lax.rem(y + step, NY)}

    def zdev(step):
        return {"seq": lax.rem(z + step, nz) * NY + y}

    def lanes(b):
        return slice(b * LANE, (b + 1) * LANE)

    g, btw = gath.at[1, 0], gath.at[0, 0]
    own_x = ext.at[pl.ds(32, rows)]

    loads = []
    for i, (src, dst) in enumerate(
        [
            (x_in.at[0], own_x),
            (kw_in, kw),
            (mix_in.at[0, 0], mix.at[0]),
            (cot_in.at[0], cot),
            (mix_in.at[0, 1], mix.at[1]),
            (head_in, head),
            (lab_in, lab),
            (ev_in, ev),
        ]
    ):
        copy = pltpu.make_async_copy(src, dst, lsem.at[i])
        copy.start()
        loads.append(copy)

    sends = []

    def push(src, dst, target):
        n = len(sends)
        copy = pltpu.make_async_remote_copy(
            src_ref=src,
            dst_ref=dst,
            send_sem=ssem.at[n],
            recv_sem=rsem.at[n],
            device_id=target,
            device_id_type=MESH,
        )
        copy.start()
        sends.append(copy)
        return copy

    def got(copies):
        for c in copies:
            c.wait_recv()

    barrier = pltpu.get_barrier_semaphore()
    greet = [seq(-1), seq(-2), seq(1), seq(2)]
    greet += [ydev(j) for j in range(1, NY)] + [zdev(j) for j in range(1, nz)]
    greet.append({"section": lax.rem(sec + 1, nsec)})
    for target in greet:
        pl.semaphore_signal(barrier, inc=1, device_id=target, device_id_type=MESH)
    pl.semaphore_wait(barrier, len(greet))

    def share(src, dst):
        return [push(src(j), dst(j), ydev(j)) for j in range(1, NY)]

    def gather_near(own, slot):
        return [push(own, slot(1), ydev(1)), push(own, slot(NY - 1), ydev(NY - 1))]

    def gather_far(copies, slot):
        on = []
        for copy, j, at in ((copies[0], 1, 0), (copies[1], NY - 1, rows // 2)):
            got([copy])
            part = pl.ds(at, rows // 2)
            on.append(push(slot(j).at[part], slot(2).at[part], ydev(j)))
        return on

    loads[0].wait()
    halo = [push(ext.at[pl.ds(rows, 32)], ext.at[pl.ds(0, 32)], seq(1))]
    loads[3].wait()
    cots = gather_near(cot, lambda j: gath.at[1, j])
    g[...] = cot[...]

    loads[1].wait()
    expand_weights(kw, 0, wbd.at[0], groups)
    loads[2].wait()
    got(halo)

    @pl.when(q == 0)
    def _():
        ext[0:32] = jnp.zeros((32, chans), BF)

    def taps_short(b):
        return jnp.concatenate(
            [ext[32 : 32 + rows, lanes(b)], ext[16 : 16 + rows, lanes(b)], ext[0:rows, lanes(b)]],
            axis=1,
        )

    def taps_long(b):
        return jnp.concatenate([mid[i, :, lanes(b)] for i in range(3)], axis=1)

    def gates(layer, taps):
        for b in range(blocks):
            pre = mm(taps(b), wbd[layer, b], NN).astype(BF).astype(F32)
            filt = jnp.tanh(pre[:, :LANE])
            gate = jax.nn.sigmoid(pre[:, LANE:])
            gated[layer, :, lanes(b)] = (filt * gate).astype(BF)
            fac[layer, 0, :, lanes(b)] = gate * (1.0 - filt * filt)
            fac[layer, 1, :, lanes(b)] = filt * gate * (1.0 - gate)

    def turn(layer):
        for b in range(blocks):
            turned = gated[layer, :, lanes(b)].T
            for i in range(per):
                d = b * per + i
                slc_s[layer, d % NY, d // NY] = turned[i * rd : (i + 1) * rd]

    def share_slices(layer):
        slc_r[layer, 0] = slc_s[layer, y]
        return share(
            lambda j: slc_s.at[layer, lax.rem(y + j, NY)], lambda j: slc_r.at[layer, j]
        )

    gates(0, taps_short)
    mid[0] = (ext[32 : 32 + rows].astype(F32) + mm(gated[0], mix[0], NN)).astype(BF)
    forth = [push(mid.at[0], mid.at[2], seq(NY)), push(mid.at[0], mid.at[1], seq(2))]

    cots = gather_far(cots, lambda j: gath.at[1, j])
    turn(0)
    slices0 = share_slices(0)
    expand_weights(kw, 1, wbd.at[1], groups)
    for copy in loads[4:]:
        copy.wait()
    got(forth)

    @pl.when(q < 2)
    def _():
        mid[1] = jnp.zeros((rows, chans), BF)

    @pl.when(q < NY)
    def _():
        mid[2] = jnp.zeros((rows, chans), BF)

    gates(1, taps_long)

    def add_loss(ref, grad):
        ref[...] = (ref[...].astype(F32) + mm(grad, head[...], TN)).astype(BF)

    dlog[0] = jnp.zeros(dlog.shape[1:], BF)

    @pl.when(last)
    def _():
        top = (mid[0].astype(F32) + mm(gated[1], mix[1], NN)).astype(BF)
        hazard = jax.nn.sigmoid(mm(head[...], top, NT))
        bins = iota(hazard.shape, 0)
        below = jnp.where(bins <= lab[...], hazard, 0.0)
        at_label = jnp.where(bins == lab[...], ev[...].astype(F32), 0.0)
        dlog[0] = (below - at_label).astype(BF)
        add_loss(g, dlog[0])

    losses = share(lambda j: dlog.at[0], lambda j: dlog.at[j])

    def cot_of_pre(layer, upstream):
        dgated = mm(upstream, mix[layer], NT)
        for b in range(blocks):
            both = jnp.concatenate(
                [
                    dgated[:, lanes(b)] * fac[layer, 0, :, lanes(b)],
                    dgated[:, lanes(b)] * fac[layer, 1, :, lanes(b)],
                ],
                axis=1,
            ).astype(BF)
            dpre[layer, :, 256 * b : 256 * (b + 1)] = both

    def back_taps(layer, b):
        return mm(dpre[layer, :, 256 * b : 256 * (b + 1)], wbd[layer, b], NT)

    cot_of_pre(1, g[...])
    for b in range(blocks):
        prods = back_taps(1, b)
        acc[:, lanes(b)] = prods[:, :LANE]
        snd_n[:, lanes(b)] = prods[:, LANE : 2 * LANE].astype(BF)
        snd_f[:, lanes(b)] = prods[:, 2 * LANE :].astype(BF)
    back = [push(snd_f, rcv_f, seq(-NY)), push(snd_n, rcv_n, seq(-2))]
    turn(1)
    slices1 = share_slices(1)

    compact = jnp.where(
        iota((768, LANE), 1) == 32 * (iota((768, LANE), 0) >> 8) + out_channel(iota((768, LANE), 0) & 255),
        1.0,
        0.0,
    ).astype(BF)
    own_group = (iota((LANE, 256), 0) >> 4) == ((iota((LANE, 256), 1) & 127) >> 4)

    def conv_terms(layer, taps):
        for b in range(blocks):
            full = mm(taps(b), dpre[layer, :, 256 * b : 256 * (b + 1)], TN)
            kept = jnp.concatenate(
                [
                    jnp.where(own_group, full[k * LANE : (k + 1) * LANE], 0.0).astype(BF)
                    for k in range(3)
                ],
                axis=1,
            )
            packed = mm(kept, compact, NN).astype(BF)
            for i in range(per):
                d = b * per + i
                cnv_s[layer, d % NY, d // NY] = packed[i * rd : (i + 1) * rd]
        return share(
            lambda j: cnv_s.at[layer, lax.rem(y + j, NY)], lambda j: cnv_r.at[layer, j - 1]
        )

    convs1 = conv_terms(1, taps_long)

    def quarter(layer, lo, w):
        left = jnp.concatenate(
            [slc_r[layer, j].reshape(nz * rd, rows) for j in range(NY)], axis=1
        )
        right = gath[layer, :, :, lo : lo + w].reshape(NY * rows, w)
        return mm(left, right, NN).reshape(nz, rd, w)

    def spread(buf, dst):
        return [
            push(buf.at[lax.rem(z + j, nz)], dst.at[j - 1], zdev(j)) for j in range(1, nz)
        ]

    got(slices1)
    got(cots)
    got(losses)
    for copy in cots:
        copy.wait_send()

    @pl.when(last)
    def _():
        for j in range(1, NY):
            add_loss(gath.at[1, j], dlog[j])

    def ring(own, done):
        right_s, right_r, left_s, left_r = ring_bufs
        arrived, at = None, 0
        for t in range(1, nz // 2 + 1):
            dist = nz // 2 - t + 1
            to_r, to_l = lax.rem(z + dist, nz), lax.rem(z - dist + nz, nz)
            size = 1 if t == 1 else 2
            if arrived is not None:
                was, copies = arrived
                got(copies)
            for d in range(2):
                if t > 1 or d == 0:
                    v = own(to_r, d)
                    if t > 2 or (t == 2 and d == 0):
                        v = v + right_r[was + d].astype(F32)
                    right_s[at + d] = v.astype(BF)
                if t > 1 or d == 1:
                    v = own(to_l, d)
                    if t > 2 or (t == 2 and d == 1):
                        v = v + left_r[was + (0 if t == 2 else d)].astype(F32)
                    left_s[at + (0 if t == 1 else d)] = v.astype(BF)
            copies = [
                push(right_s.at[pl.ds(at, size)], right_r.at[pl.ds(at, size)], zdev(1)),
                push(left_s.at[pl.ds(at, size)], left_r.at[pl.ds(at, size)], zdev(nz - 1)),
            ]
            arrived = (at, copies)
            at += size
            yield
        was, copies = arrived
        got(copies)
        for d in range(2):
            v = own(z, d)
            if nz > 2:
                v = v + right_r[was + d].astype(F32) + left_r[was + d].astype(F32)
            elif d == 0:
                v = v + right_r[was].astype(F32)
            else:
                v = v + left_r[was].astype(F32)
            done(d, v)
        yield

    half = rd // 2
    for lo in range(0, chans, 256):
        zown[1, :, :, lo : lo + 256] = quarter(1, lo, 256)

    def conv_sum(layer, copies):
        got(copies)
        sums = cnv_s[layer, y].astype(F32)
        for j in range(NY - 1):
            sums = sums + cnv_r[layer, j].astype(F32)
        zown[layer, :, :, chans : chans + LANE] = sums
        return sums

    def put_conv(layer, lo, sums):
        for k in range(3):
            cg_out[0, layer, k, lo // 16 : (lo + sums.shape[0]) // 16] = sums[
                :, 32 * k : 32 * (k + 1)
            ].reshape(sums.shape[0] // 16, 16, 32)

    def finish1(d, v):
        mg_out[0, d * half : (d + 1) * half, 1, :] = v[:, 0:chans]
        put_conv(1, d * half, v[:, chans:])

    conv_sum(1, convs1)
    ring1 = ring(lambda e, d: zown[1, e, d * half : (d + 1) * half, :], finish1)
    next(ring1, None)

    got(back)

    @pl.when(q >= nq - 2)
    def _():
        rcv_n[...] = jnp.zeros((rows, chans), BF)

    @pl.when(q >= nq - NY)
    def _():
        rcv_f[...] = jnp.zeros((rows, chans), BF)

    btw[...] = (
        g[...].astype(F32) + acc[...] + rcv_n[...].astype(F32) + rcv_f[...].astype(F32)
    ).astype(BF)
    def lane_slot(lo, w):
        return lambda j: gath.at[0, j, :, pl.ds(lo, w)]

    slots = [lane_slot(lo, w) for lo, w, _ in chunks]
    shared = [gather_near(slot(0), slot) for slot in slots]
    next(ring1, None)
    cot_of_pre(0, btw[...])
    for b in range(blocks):
        prods = back_taps(0, b)
        acc[:, lanes(b)] = prods[:, :LANE]
        tap1[0:rows, lanes(b)] = prods[:, LANE : 2 * LANE]
        tap2[0:rows, lanes(b)] = prods[:, 2 * LANE :]
    hal_s[0:16] = tap2[0:16].astype(BF)
    hal_s[16:32] = (tap1[0:16] + tap2[16:32]).astype(BF)
    back_halo = push(hal_s, hal_r, seq(-1))
    shared[0] = gather_far(shared[0], slots[0])
    convs0 = conv_terms(0, taps_short)
    shared[1] = gather_far(shared[1], slots[1])
    next(ring1, None)
    tap1[rows : rows + 16] = jnp.zeros((16, chans), F32)
    tap2[rows : rows + 32] = jnp.zeros((32, chans), F32)
    back_halo.wait_recv()

    @pl.when(q == nq - 1)
    def _():
        hal_r[...] = jnp.zeros((32, chans), BF)

    total = btw[...].astype(F32) + acc[...] + tap1[16 : 16 + rows] + tap2[32 : 32 + rows]
    ig_out[0, 0 : rows - 32] = total[0 : rows - 32].astype(BF)
    ig_out[0, rows - 32 : rows] = (total[rows - 32 :] + hal_r[...].astype(F32)).astype(BF)
    to_prev = push(ig_out.at[0], nxt, {"section": lax.rem(sec + nsec - 1, nsec)})

    for c in range(2, len(chunks)):
        shared[c] = gather_far(shared[c], slots[c])
    got(slices0)
    over0 = []
    for c, (lo, w, conv) in enumerate(chunks):
        got(shared[c])
        block = quarter(0, lo, w)
        zown[0, :, :, lo : lo + w] = block
        zs0[c][:, :, 0:w] = block.astype(BF)
        if conv:
            zs0[c][:, :, w : w + LANE] = conv_sum(0, convs0).astype(BF)
        over0.append(spread(zs0[c], zr0[c]))
        if c == 0:
            next(ring1, None)
    for _ in range(nz // 2 - 3):
        next(ring1, None)

    def total_of(own, bufs, lo, w):
        v = own
        for j in range(nz - 1):
            v = v + bufs[j, :, lo : lo + w].astype(F32)
        return v

    to_prev.wait_recv()

    @pl.when(last)
    def _():
        nc_out[0] = g[...]

    @pl.when(jnp.logical_not(last))
    def _():
        nc_out[0] = nxt[...]

    for c, (lo, w, conv) in enumerate(chunks):
        got(over0[c])
        mg_out[0, :, 0, lo : lo + w] = total_of(zown[0, z, :, lo : lo + w], zr0[c], 0, w)
        if conv:
            put_conv(0, 0, total_of(zown[0, z, :, chans : chans + LANE], zr0[c], w, LANE))

    for copy in sends:
        if all(copy is not c for c in cots):
            copy.wait_send()


def hand_over(*refs):
    srcs, dsts, bufs, (sem_in, sem_out) = refs[:4], refs[4:8], refs[8:12], refs[12:]
    fetch = [pltpu.make_async_copy(a, b, sem_in.at[i]) for i, (a, b) in enumerate(zip(srcs, bufs))]
    store = [pltpu.make_async_copy(a, b, sem_out.at[i]) for i, (a, b) in enumerate(zip(bufs, dsts))]
    for copy in fetch:
        copy.start()
    for before, after in zip(fetch, store):
        before.wait()
        after.start()
    for copy in store:
        copy.wait()


def solution(mesh):
    nsec, nq = mesh.shape["section"], mesh.shape["seq"]
    nz = nq // NY

    def body(x, cot, kernel_weight, blend, head, labels, events):
        _, rows, chans = x.shape
        groups, gin, gout = kernel_weight.shape[3:]
        rd = chans // nq
        blocks = chans // LANE
        kw = jnp.transpose(kernel_weight[0], (0, 1, 3, 4, 2)).reshape(6, gin * gout, groups)
        any_ = pl.BlockSpec(memory_space=pl.ANY)
        vm = pl.BlockSpec(memory_space=pltpu.VMEM)
        act = pltpu.VMEM((rows, chans), BF)
        quarter = chans // 4
        chunks = [(0, 2 * quarter, False), (2 * quarter, quarter, False), (3 * quarter, quarter, True)]
        wide = [w + (LANE if conv else 0) for _, w, conv in chunks]
        n_push = 1 + 4 + 2 + 6 + 3 + 2 + 6 + nz + 16 + 2 + 4 * (nz - 1)
        bins = head.shape[1]
        scratch = [
            pltpu.VMEM((rows + 32, chans), BF),
            act,
            pltpu.VMEM((6, gin * gout, groups), BF),
            pltpu.VMEM((2, chans, chans), BF),
            pltpu.VMEM((bins, chans), BF),
            pltpu.VMEM((1, rows), jnp.int32),
            pltpu.VMEM((1, rows), jnp.int32),
            pltpu.VMEM((2, blocks, 3 * LANE, 2 * LANE), BF),
            pltpu.VMEM((2, rows, chans), BF),
            pltpu.VMEM((2, 2, rows, chans), F32),
            pltpu.VMEM((3, rows, chans), BF),
            pltpu.VMEM((2, rows, 2 * chans), BF),
            pltpu.VMEM((rows, chans), F32),
            act,
            act,
            act,
            act,
            pltpu.VMEM((rows + 16, chans), F32),
            pltpu.VMEM((rows + 32, chans), F32),
            pltpu.VMEM((32, chans), BF),
            pltpu.VMEM((32, chans), BF),
            act,
            pltpu.VMEM((2, NY, rows, chans), BF),
            pltpu.VMEM((2, NY, nz, rd, rows), BF),
            pltpu.VMEM((2, NY, nz, rd, rows), BF),
            pltpu.VMEM((NY, bins, rows), BF),
            pltpu.VMEM((2, NY, nz, rd, LANE), BF),
            pltpu.VMEM((2, NY - 1, nz, rd, LANE), BF),
            pltpu.VMEM((2, nz, rd, chans + LANE), F32),
            pltpu.SemaphoreType.DMA((8,)),
            pltpu.SemaphoreType.DMA((n_push,)),
            pltpu.SemaphoreType.DMA((n_push,)),
        ]
        scratch += [pltpu.VMEM((nz, rd, w), BF) for w in wide]
        scratch += [pltpu.VMEM((nz - 1, rd, w), BF) for w in wide]
        scratch += [pltpu.VMEM((nz - 1, rd // 2, chans + LANE), BF)] * 4
        shapes = (
            jax.ShapeDtypeStruct((1, rows, chans), BF),
            jax.ShapeDtypeStruct((1, rows, chans), BF),
            jax.ShapeDtypeStruct((1, rd, 2, chans), F32),
            jax.ShapeDtypeStruct((1, 2, 3, groups // nq, gin, gout), F32),
        )
        outs = pl.pallas_call(
            functools.partial(kernel, nz, nsec, chunks),
            out_shape=shapes,
            in_specs=[any_] * 7,
            out_specs=(vm, vm, vm, vm),
            scratch_shapes=scratch,
            compiler_params=pltpu.CompilerParams(
                collective_id=0, has_side_effects=True, vmem_limit_bytes=58 * 1024 * 1024
            ),
        )(x, cot, kw, blend, head.T, labels.reshape(1, rows), events.reshape(1, rows))
        return pl.pallas_call(
            hand_over,
            out_shape=shapes,
            in_specs=[any_] * 4,
            out_specs=(any_,) * 4,
            scratch_shapes=[pltpu.VMEM(o.shape, o.dtype) for o in shapes]
            + [pltpu.SemaphoreType.DMA((4,))] * 2,
        )(*outs)

    return jax.shard_map(
        body,
        mesh=mesh,
        in_specs=(
            P("section", "seq", None),
            P("section", "seq", None),
            P("section", None, None, None, None, None),
            P("section", None, None, None),
            P(),
            P("seq"),
            P("seq"),
        ),
        out_specs=(
            P("section", "seq", None),
            P("section", "seq", None),
            P("section", "seq", None, None),
            P("section", None, None, "seq", None, None),
        ),
        check_vma=False,
    )
```

```python
import functools

import jax
import jax.numpy as jnp
from jax import lax
from jax.experimental import pallas as pl
from jax.experimental.pallas import tpu as pltpu
from jax.sharding import PartitionSpec as P

MESH = pl.DeviceIdType.MESH
F32 = jnp.float32
BF = jnp.bfloat16
NY = 4
LANE = 128

NT = (((1,), (1,)), ((), ()))
TN = (((0,), (0,)), ((), ()))
NN = (((1,), (0,)), ((), ()))


def mm(a, b, dims):
    return lax.dot_general(a, b, dims, preferred_element_type=F32)


def iota(shape, dim):
    return lax.broadcasted_iota(jnp.int32, shape, dim)


def out_channel(col):
    return jnp.where(col < LANE, col & 15, 16 + (col & 15))


def expand_weights(kw, layer, wbd, groups):
    half = groups * 16 // 2
    sel = jnp.where(
        out_channel(iota((512, 256), 1)) == (iota((512, 256), 0) & 31), 1.0, 0.0
    ).astype(BF)
    keep_in = (iota((half, 512), 1) >> 5) == (iota((half, 512), 0) & 15)
    keep_group = ((iota((half, 256), 0) >> 4) & 7) == ((iota((half, 256), 1) & 127) >> 4)
    for part in range(2):
        pick = jnp.where(
            (iota((half, groups), 0) >> 4) + part * (groups // 2) == iota((half, groups), 1),
            1.0,
            0.0,
        ).astype(BF)
        for k in range(3):
            rows = mm(pick, kw[3 * layer + k], NT)
            rows = jnp.where(keep_in, rows, 0.0).astype(BF)
            full = jnp.where(keep_group, mm(rows, sel, NN), 0.0).astype(BF)
            for b in range(half // LANE):
                wbd[part * (half // LANE) + b, k * LANE : (k + 1) * LANE, :] = full[
                    b * LANE : (b + 1) * LANE
                ]


def kernel(nz, nsec, chunks, *refs):
    (x_in, cot_in, kw_in, mix_in, head_in, lab_in, ev_in) = refs[:7]
    (ig_out, nc_out, mg_out, cg_out) = refs[7:11]
    (ext, cot, kw, mix, head, lab, ev, wbd, gated, fac, mid, dpre, acc, snd_n, snd_f, rcv_n, rcv_f,
     tap1, tap2, hal_s, hal_r, nxt, gath, slc_s, slc_r, dlog, cnv_s, cnv_r, zown,
     lsem, ssem, rsem, ig_buf, nc_buf, mg_buf, cg_buf, osem) = refs[11:48]
    zs0, zr0 = refs[48 : 48 + len(chunks)], refs[48 + len(chunks) : 48 + 2 * len(chunks)]
    ring_bufs = refs[48 + 2 * len(chunks) :]

    _, rows, chans = mid.shape
    nq = NY * nz
    rd = chans // nq
    blocks = chans // LANE
    per = LANE // rd
    groups = chans // 16
    sec = lax.axis_index("section")
    q = lax.axis_index("seq")
    y = lax.rem(q, NY)
    z = q // NY
    last = sec == nsec - 1

    def seq(step):
        return {"seq": lax.rem(q + step + nq, nq)}

    def ydev(step):
        return {"seq": z * NY + lax.rem(y + step, NY)}

    def zdev(step):
        return {"seq": lax.rem(z + step, nz) * NY + y}

    def lanes(b):
        return slice(b * LANE, (b + 1) * LANE)

    g, btw = gath.at[1, 0], gath.at[0, 0]
    own_x = ext.at[pl.ds(32, rows)]

    loads = []
    for i, (src, dst) in enumerate(
        [
            (x_in.at[0], own_x),
            (kw_in, kw),
            (mix_in.at[0, 0], mix.at[0]),
            (cot_in.at[0], cot),
            (mix_in.at[0, 1], mix.at[1]),
            (head_in, head),
            (lab_in, lab),
            (ev_in, ev),
        ]
    ):
        copy = pltpu.make_async_copy(src, dst, lsem.at[i])
        copy.start()
        loads.append(copy)

    sends = []

    def push(src, dst, target):
        n = len(sends)
        copy = pltpu.make_async_remote_copy(
            src_ref=src,
            dst_ref=dst,
            send_sem=ssem.at[n],
            recv_sem=rsem.at[n],
            device_id=target,
            device_id_type=MESH,
        )
        copy.start()
        sends.append(copy)
        return copy

    def got(copies):
        for c in copies:
            c.wait_recv()

    barrier = pltpu.get_barrier_semaphore()
    greet = [seq(-1), seq(-2), seq(1), seq(2)]
    greet += [ydev(j) for j in range(1, NY)] + [zdev(j) for j in range(1, nz)]
    greet.append({"section": lax.rem(sec + 1, nsec)})
    for target in greet:
        pl.semaphore_signal(barrier, inc=1, device_id=target, device_id_type=MESH)
    pl.semaphore_wait(barrier, len(greet))

    def share(src, dst):
        return [push(src(j), dst(j), ydev(j)) for j in range(1, NY)]

    def gather_near(own, slot):
        return [push(own, slot(1), ydev(1)), push(own, slot(NY - 1), ydev(NY - 1))]

    def gather_far(copies, slot):
        on = []
        for copy, j, at in ((copies[0], 1, 0), (copies[1], NY - 1, rows // 2)):
            got([copy])
            part = pl.ds(at, rows // 2)
            on.append(push(slot(j).at[part], slot(2).at[part], ydev(j)))
        return on

    loads[0].wait()
    halo = [push(ext.at[pl.ds(rows, 32)], ext.at[pl.ds(0, 32)], seq(1))]
    loads[3].wait()
    cots = gather_near(cot, lambda j: gath.at[1, j])
    g[...] = cot[...]

    loads[1].wait()
    expand_weights(kw, 0, wbd.at[0], groups)
    loads[2].wait()
    got(halo)

    @pl.when(q == 0)
    def _():
        ext[0:32] = jnp.zeros((32, chans), BF)

    def taps_short(b):
        return jnp.concatenate(
            [ext[32 : 32 + rows, lanes(b)], ext[16 : 16 + rows, lanes(b)], ext[0:rows, lanes(b)]],
            axis=1,
        )

    def taps_long(b):
        return jnp.concatenate([mid[i, :, lanes(b)] for i in range(3)], axis=1)

    def gates(layer, taps):
        for b in range(blocks):
            pre = mm(taps(b), wbd[layer, b], NN).astype(BF).astype(F32)
            filt = jnp.tanh(pre[:, :LANE])
            gate = jax.nn.sigmoid(pre[:, LANE:])
            gated[layer, :, lanes(b)] = (filt * gate).astype(BF)
            fac[layer, 0, :, lanes(b)] = gate * (1.0 - filt * filt)
            fac[layer, 1, :, lanes(b)] = filt * gate * (1.0 - gate)

    def turn(layer):
        for b in range(blocks):
            turned = gated[layer, :, lanes(b)].T
            for i in range(per):
                d = b * per + i
                slc_s[layer, d % NY, d // NY] = turned[i * rd : (i + 1) * rd]

    def share_slices(layer):
        slc_r[layer, 0] = slc_s[layer, y]
        return share(
            lambda j: slc_s.at[layer, lax.rem(y + j, NY)], lambda j: slc_r.at[layer, j]
        )

    gates(0, taps_short)
    mid[0] = (ext[32 : 32 + rows].astype(F32) + mm(gated[0], mix[0], NN)).astype(BF)
    forth = [push(mid.at[0], mid.at[2], seq(NY)), push(mid.at[0], mid.at[1], seq(2))]

    cots = gather_far(cots, lambda j: gath.at[1, j])
    turn(0)
    slices0 = share_slices(0)
    expand_weights(kw, 1, wbd.at[1], groups)
    for copy in loads[4:]:
        copy.wait()
    got(forth)

    @pl.when(q < 2)
    def _():
        mid[1] = jnp.zeros((rows, chans), BF)

    @pl.when(q < NY)
    def _():
        mid[2] = jnp.zeros((rows, chans), BF)

    gates(1, taps_long)

    def add_loss(ref, grad):
        ref[...] = (ref[...].astype(F32) + mm(grad, head[...], TN)).astype(BF)

    dlog[0] = jnp.zeros(dlog.shape[1:], BF)

    @pl.when(last)
    def _():
        top = (mid[0].astype(F32) + mm(gated[1], mix[1], NN)).astype(BF)
        hazard = jax.nn.sigmoid(mm(head[...], top, NT))
        bins = iota(hazard.shape, 0)
        below = jnp.where(bins <= lab[...], hazard, 0.0)
        at_label = jnp.where(bins == lab[...], ev[...].astype(F32), 0.0)
        dlog[0] = (below - at_label).astype(BF)
        add_loss(g, dlog[0])

    losses = share(lambda j: dlog.at[0], lambda j: dlog.at[j])

    def cot_of_pre(layer, upstream):
        dgated = mm(upstream, mix[layer], NT)
        for b in range(blocks):
            both = jnp.concatenate(
                [
                    dgated[:, lanes(b)] * fac[layer, 0, :, lanes(b)],
                    dgated[:, lanes(b)] * fac[layer, 1, :, lanes(b)],
                ],
                axis=1,
            ).astype(BF)
            dpre[layer, :, 256 * b : 256 * (b + 1)] = both

    def back_taps(layer, b):
        return mm(dpre[layer, :, 256 * b : 256 * (b + 1)], wbd[layer, b], NT)

    cot_of_pre(1, g[...])
    for b in range(blocks):
        prods = back_taps(1, b)
        acc[:, lanes(b)] = prods[:, :LANE]
        snd_n[:, lanes(b)] = prods[:, LANE : 2 * LANE].astype(BF)
        snd_f[:, lanes(b)] = prods[:, 2 * LANE :].astype(BF)
    back = [push(snd_f, rcv_f, seq(-NY)), push(snd_n, rcv_n, seq(-2))]
    turn(1)
    slices1 = share_slices(1)

    compact = jnp.where(
        iota((768, LANE), 1) == 32 * (iota((768, LANE), 0) >> 8) + out_channel(iota((768, LANE), 0) & 255),
        1.0,
        0.0,
    ).astype(BF)
    own_group = (iota((LANE, 256), 0) >> 4) == ((iota((LANE, 256), 1) & 127) >> 4)

    def conv_terms(layer, taps):
        for b in range(blocks):
            full = mm(taps(b), dpre[layer, :, 256 * b : 256 * (b + 1)], TN)
            kept = jnp.concatenate(
                [
                    jnp.where(own_group, full[k * LANE : (k + 1) * LANE], 0.0).astype(BF)
                    for k in range(3)
                ],
                axis=1,
            )
            packed = mm(kept, compact, NN).astype(BF)
            for i in range(per):
                d = b * per + i
                cnv_s[layer, d % NY, d // NY] = packed[i * rd : (i + 1) * rd]
        return share(
            lambda j: cnv_s.at[layer, lax.rem(y + j, NY)], lambda j: cnv_r.at[layer, j - 1]
        )

    convs1 = conv_terms(1, taps_long)

    def quarter(layer, lo, w):
        left = jnp.concatenate(
            [slc_r[layer, j].reshape(nz * rd, rows) for j in range(NY)], axis=1
        )
        right = gath[layer, :, :, lo : lo + w].reshape(NY * rows, w)
        return mm(left, right, NN).reshape(nz, rd, w)

    def spread(buf, dst):
        return [
            push(buf.at[lax.rem(z + j, nz)], dst.at[j - 1], zdev(j)) for j in range(1, nz)
        ]

    got(slices1)
    got(cots)
    got(losses)
    for copy in cots:
        copy.wait_send()

    @pl.when(last)
    def _():
        for j in range(1, NY):
            add_loss(gath.at[1, j], dlog[j])

    def ring(own, done):
        right_s, right_r, left_s, left_r = ring_bufs
        arrived, at = None, 0
        for t in range(1, nz // 2 + 1):
            dist = nz // 2 - t + 1
            to_r, to_l = lax.rem(z + dist, nz), lax.rem(z - dist + nz, nz)
            size = 1 if t == 1 else 2
            if arrived is not None:
                was, copies = arrived
                got(copies)
            for d in range(2):
                if t > 1 or d == 0:
                    v = own(to_r, d)
                    if t > 2 or (t == 2 and d == 0):
                        v = v + right_r[was + d].astype(F32)
                    right_s[at + d] = v.astype(BF)
                if t > 1 or d == 1:
                    v = own(to_l, d)
                    if t > 2 or (t == 2 and d == 1):
                        v = v + left_r[was + (0 if t == 2 else d)].astype(F32)
                    left_s[at + (0 if t == 1 else d)] = v.astype(BF)
            copies = [
                push(right_s.at[pl.ds(at, size)], right_r.at[pl.ds(at, size)], zdev(1)),
                push(left_s.at[pl.ds(at, size)], left_r.at[pl.ds(at, size)], zdev(nz - 1)),
            ]
            arrived = (at, copies)
            at += size
            yield
        was, copies = arrived
        got(copies)
        for d in range(2):
            v = own(z, d)
            if nz > 2:
                v = v + right_r[was + d].astype(F32) + left_r[was + d].astype(F32)
            elif d == 0:
                v = v + right_r[was].astype(F32)
            else:
                v = v + left_r[was].astype(F32)
            done(d, v)
        yield

    half = rd // 2
    for lo in range(0, chans, 256):
        zown[1, :, :, lo : lo + 256] = quarter(1, lo, 256)

    def conv_sum(layer, copies):
        got(copies)
        sums = cnv_s[layer, y].astype(F32)
        for j in range(NY - 1):
            sums = sums + cnv_r[layer, j].astype(F32)
        zown[layer, :, :, chans : chans + LANE] = sums
        return sums

    def put_conv(layer, lo, sums):
        for k in range(3):
            cg_buf[0, layer, k, lo // 16 : (lo + sums.shape[0]) // 16] = sums[
                :, 32 * k : 32 * (k + 1)
            ].reshape(sums.shape[0] // 16, 16, 32)

    def finish1(d, v):
        mg_buf[0, d * half : (d + 1) * half, 1, :] = v[:, 0:chans]
        put_conv(1, d * half, v[:, chans:])

    conv_sum(1, convs1)
    ring1 = ring(lambda e, d: zown[1, e, d * half : (d + 1) * half, :], finish1)
    next(ring1, None)

    got(back)

    @pl.when(q >= nq - 2)
    def _():
        rcv_n[...] = jnp.zeros((rows, chans), BF)

    @pl.when(q >= nq - NY)
    def _():
        rcv_f[...] = jnp.zeros((rows, chans), BF)

    btw[...] = (
        g[...].astype(F32) + acc[...] + rcv_n[...].astype(F32) + rcv_f[...].astype(F32)
    ).astype(BF)
    def lane_slot(lo, w):
        return lambda j: gath.at[0, j, :, pl.ds(lo, w)]

    slots = [lane_slot(lo, w) for lo, w, _ in chunks]
    shared = [gather_near(slot(0), slot) for slot in slots]
    next(ring1, None)
    cot_of_pre(0, btw[...])
    for b in range(blocks):
        prods = back_taps(0, b)
        acc[:, lanes(b)] = prods[:, :LANE]
        tap1[0:rows, lanes(b)] = prods[:, LANE : 2 * LANE]
        tap2[0:rows, lanes(b)] = prods[:, 2 * LANE :]
    hal_s[0:16] = tap2[0:16].astype(BF)
    hal_s[16:32] = (tap1[0:16] + tap2[16:32]).astype(BF)
    back_halo = push(hal_s, hal_r, seq(-1))
    shared[0] = gather_far(shared[0], slots[0])
    convs0 = conv_terms(0, taps_short)
    shared[1] = gather_far(shared[1], slots[1])
    next(ring1, None)
    tap1[rows : rows + 16] = jnp.zeros((16, chans), F32)
    tap2[rows : rows + 32] = jnp.zeros((32, chans), F32)
    back_halo.wait_recv()

    @pl.when(q == nq - 1)
    def _():
        hal_r[...] = jnp.zeros((32, chans), BF)

    total = btw[...].astype(F32) + acc[...] + tap1[16 : 16 + rows] + tap2[32 : 32 + rows]
    ig_buf[0, 0 : rows - 32] = total[0 : rows - 32].astype(BF)
    ig_buf[0, rows - 32 : rows] = (total[rows - 32 :] + hal_r[...].astype(F32)).astype(BF)
    def write(i, src, dst):
        copy = pltpu.make_async_copy(src, dst, osem.at[i])
        copy.start()
        return copy

    writes = [write(0, ig_buf, ig_out)]
    to_prev = push(ig_buf.at[0], nxt, {"section": lax.rem(sec + nsec - 1, nsec)})

    for c in range(2, len(chunks)):
        shared[c] = gather_far(shared[c], slots[c])
    got(slices0)
    over0 = []
    for c, (lo, w, conv) in enumerate(chunks):
        got(shared[c])
        block = quarter(0, lo, w)
        zown[0, :, :, lo : lo + w] = block
        zs0[c][:, :, 0:w] = block.astype(BF)
        if conv:
            zs0[c][:, :, w : w + LANE] = conv_sum(0, convs0).astype(BF)
        over0.append(spread(zs0[c], zr0[c]))
        if c == 0:
            next(ring1, None)
    for _ in range(nz // 2 - 3):
        next(ring1, None)

    def total_of(own, bufs, lo, w):
        v = own
        for j in range(nz - 1):
            v = v + bufs[j, :, lo : lo + w].astype(F32)
        return v

    to_prev.wait_recv()

    @pl.when(last)
    def _():
        nc_buf[0] = g[...]

    @pl.when(jnp.logical_not(last))
    def _():
        nc_buf[0] = nxt[...]

    writes.append(write(1, nc_buf, nc_out))

    for c, (lo, w, conv) in enumerate(chunks):
        got(over0[c])
        mg_buf[0, :, 0, lo : lo + w] = total_of(zown[0, z, :, lo : lo + w], zr0[c], 0, w)
        if conv:
            put_conv(0, 0, total_of(zown[0, z, :, chans : chans + LANE], zr0[c], w, LANE))

    writes += [write(2, mg_buf, mg_out), write(3, cg_buf, cg_out)]
    for copy in writes:
        copy.wait()
    for copy in sends:
        if all(copy is not c for c in cots):
            copy.wait_send()


def hand_over(*refs):
    srcs, dsts, bufs, (sem_in, sem_out) = refs[:4], refs[4:8], refs[8:12], refs[12:]
    fetch = [pltpu.make_async_copy(a, b, sem_in.at[i]) for i, (a, b) in enumerate(zip(srcs, bufs))]
    store = [pltpu.make_async_copy(a, b, sem_out.at[i]) for i, (a, b) in enumerate(zip(bufs, dsts))]
    for copy in fetch:
        copy.start()
    for before, after in zip(fetch, store):
        before.wait()
        after.start()
    for copy in store:
        copy.wait()


def solution(mesh):
    nsec, nq = mesh.shape["section"], mesh.shape["seq"]
    nz = nq // NY

    def body(x, cot, kernel_weight, blend, head, labels, events):
        _, rows, chans = x.shape
        groups, gin, gout = kernel_weight.shape[3:]
        rd = chans // nq
        blocks = chans // LANE
        kw = jnp.transpose(kernel_weight[0], (0, 1, 3, 4, 2)).reshape(6, gin * gout, groups)
        any_ = pl.BlockSpec(memory_space=pl.ANY)
        vm = pl.BlockSpec(memory_space=pltpu.VMEM)
        act = pltpu.VMEM((rows, chans), BF)
        quarter = chans // 4
        chunks = [(0, 2 * quarter, False), (2 * quarter, quarter, False), (3 * quarter, quarter, True)]
        wide = [w + (LANE if conv else 0) for _, w, conv in chunks]
        n_push = 1 + 4 + 2 + 6 + 3 + 2 + 6 + nz + 16 + 2 + 4 * (nz - 1)
        bins = head.shape[1]
        scratch = [
            pltpu.VMEM((rows + 32, chans), BF),
            act,
            pltpu.VMEM((6, gin * gout, groups), BF),
            pltpu.VMEM((2, chans, chans), BF),
            pltpu.VMEM((bins, chans), BF),
            pltpu.VMEM((1, rows), jnp.int32),
            pltpu.VMEM((1, rows), jnp.int32),
            pltpu.VMEM((2, blocks, 3 * LANE, 2 * LANE), BF),
            pltpu.VMEM((2, rows, chans), BF),
            pltpu.VMEM((2, 2, rows, chans), F32),
            pltpu.VMEM((3, rows, chans), BF),
            pltpu.VMEM((2, rows, 2 * chans), BF),
            pltpu.VMEM((rows, chans), F32),
            act,
            act,
            act,
            act,
            pltpu.VMEM((rows + 16, chans), F32),
            pltpu.VMEM((rows + 32, chans), F32),
            pltpu.VMEM((32, chans), BF),
            pltpu.VMEM((32, chans), BF),
            act,
            pltpu.VMEM((2, NY, rows, chans), BF),
            pltpu.VMEM((2, NY, nz, rd, rows), BF),
            pltpu.VMEM((2, NY, nz, rd, rows), BF),
            pltpu.VMEM((NY, bins, rows), BF),
            pltpu.VMEM((2, NY, nz, rd, LANE), BF),
            pltpu.VMEM((2, NY - 1, nz, rd, LANE), BF),
            pltpu.VMEM((2, nz, rd, chans + LANE), F32),
            pltpu.SemaphoreType.DMA((8,)),
            pltpu.SemaphoreType.DMA((n_push,)),
            pltpu.SemaphoreType.DMA((n_push,)),
        ]
        shapes = (
            jax.ShapeDtypeStruct((1, rows, chans), BF),
            jax.ShapeDtypeStruct((1, rows, chans), BF),
            jax.ShapeDtypeStruct((1, rd, 2, chans), F32),
            jax.ShapeDtypeStruct((1, 2, 3, groups // nq, gin, gout), F32),
        )
        scratch += [pltpu.VMEM(o.shape, o.dtype) for o in shapes] + [pltpu.SemaphoreType.DMA((4,))]
        scratch += [pltpu.VMEM((nz, rd, w), BF) for w in wide]
        scratch += [pltpu.VMEM((nz - 1, rd, w), BF) for w in wide]
        scratch += [pltpu.VMEM((nz - 1, rd // 2, chans + LANE), BF)] * 4
        outs = pl.pallas_call(
            functools.partial(kernel, nz, nsec, chunks),
            out_shape=shapes,
            in_specs=[any_] * 7,
            out_specs=(any_,) * 4,
            scratch_shapes=scratch,
            compiler_params=pltpu.CompilerParams(
                collective_id=0, has_side_effects=True, vmem_limit_bytes=58 * 1024 * 1024
            ),
        )(x, cot, kw, blend, head.T, labels.reshape(1, rows), events.reshape(1, rows))
        return pl.pallas_call(
            hand_over,
            out_shape=shapes,
            in_specs=[any_] * 4,
            out_specs=(any_,) * 4,
            scratch_shapes=[pltpu.VMEM(o.shape, o.dtype) for o in shapes]
            + [pltpu.SemaphoreType.DMA((4,))] * 2,
        )(*outs)

    return jax.shard_map(
        body,
        mesh=mesh,
        in_specs=(
            P("section", "seq", None),
            P("section", "seq", None),
            P("section", None, None, None, None, None),
            P("section", None, None, None),
            P(),
            P("seq"),
            P("seq"),
        ),
        out_specs=(
            P("section", "seq", None),
            P("section", "seq", None),
            P("section", "seq", None, None),
            P("section", None, None, "seq", None, None),
        ),
        check_vma=False,
    )
```

```python
import functools

import jax
import jax.numpy as jnp
from jax import lax
from jax.experimental import pallas as pl
from jax.experimental.pallas import tpu as pltpu
from jax.sharding import PartitionSpec as P

MESH = pl.DeviceIdType.MESH
F32 = jnp.float32
BF = jnp.bfloat16
NY = 4
LANE = 128

NT = (((1,), (1,)), ((), ()))
TN = (((0,), (0,)), ((), ()))
NN = (((1,), (0,)), ((), ()))


def mm(a, b, dims):
    return lax.dot_general(a, b, dims, preferred_element_type=F32)


def iota(shape, dim):
    return lax.broadcasted_iota(jnp.int32, shape, dim)


def out_channel(col):
    return jnp.where(col < LANE, col & 15, 16 + (col & 15))


def expand_weights(kw, layer, wbd, groups):
    half = groups * 16 // 2
    sel = jnp.where(
        out_channel(iota((512, 256), 1)) == (iota((512, 256), 0) & 31), 1.0, 0.0
    ).astype(BF)
    keep_in = (iota((half, 512), 1) >> 5) == (iota((half, 512), 0) & 15)
    keep_group = ((iota((half, 256), 0) >> 4) & 7) == ((iota((half, 256), 1) & 127) >> 4)
    for part in range(2):
        pick = jnp.where(
            (iota((half, groups), 0) >> 4) + part * (groups // 2) == iota((half, groups), 1),
            1.0,
            0.0,
        ).astype(BF)
        for k in range(3):
            rows = mm(pick, kw[3 * layer + k], NT)
            rows = jnp.where(keep_in, rows, 0.0).astype(BF)
            full = jnp.where(keep_group, mm(rows, sel, NN), 0.0).astype(BF)
            for b in range(half // LANE):
                wbd[part * (half // LANE) + b, k * LANE : (k + 1) * LANE, :] = full[
                    b * LANE : (b + 1) * LANE
                ]


def kernel(nz, nsec, chunks, *refs):
    (x_in, cot_in, kw_in, mix_in, head_in, lab_in, ev_in) = refs[:7]
    (ig_out, nc_out, mg_out, cg_out) = refs[7:11]
    (ext, cot, kw, mix, head, lab, ev, wbd, gated, fac, mid, dpre, acc, snd_n, snd_f, rcv_n, rcv_f,
     tap1, tap2, hal_s, hal_r, nxt, gath, slc_s, slc_r, dlog, cnv_s, cnv_r, zown,
     lsem, ssem, rsem, ig_buf, nc_buf, mg_buf, cg_buf, osem) = refs[11:48]
    zs0, zr0 = refs[48 : 48 + len(chunks)], refs[48 + len(chunks) : 48 + 2 * len(chunks)]
    ring_bufs = refs[48 + 2 * len(chunks) :]

    _, rows, chans = mid.shape
    nq = NY * nz
    rd = chans // nq
    blocks = chans // LANE
    per = LANE // rd
    groups = chans // 16
    sec = lax.axis_index("section")
    q = lax.axis_index("seq")
    y = lax.rem(q, NY)
    z = q // NY
    last = sec == nsec - 1

    def seq(step):
        return {"seq": lax.rem(q + step + nq, nq)}

    def ydev(step):
        return {"seq": z * NY + lax.rem(y + step, NY)}

    def zdev(step):
        return {"seq": lax.rem(z + step, nz) * NY + y}

    def lanes(b):
        return slice(b * LANE, (b + 1) * LANE)

    g, btw = gath.at[1, 0], gath.at[0, 0]
    own_x = ext.at[pl.ds(32, rows)]

    loads = []
    for i, (src, dst) in enumerate(
        [
            (x_in.at[0], own_x),
            (kw_in, kw),
            (mix_in.at[0, 0], mix.at[0]),
            (cot_in.at[0], cot),
            (mix_in.at[0, 1], mix.at[1]),
            (head_in, head),
            (lab_in, lab),
            (ev_in, ev),
        ]
    ):
        copy = pltpu.make_async_copy(src, dst, lsem.at[i])
        copy.start()
        loads.append(copy)

    sends = []

    def push(src, dst, target):
        n = len(sends)
        copy = pltpu.make_async_remote_copy(
            src_ref=src,
            dst_ref=dst,
            send_sem=ssem.at[n],
            recv_sem=rsem.at[n],
            device_id=target,
            device_id_type=MESH,
        )
        copy.start()
        sends.append(copy)
        return copy

    def got(copies):
        for c in copies:
            c.wait_recv()

    barrier = pltpu.get_barrier_semaphore()
    greet = [seq(-1), seq(-2), seq(1), seq(2)]
    greet += [ydev(j) for j in range(1, NY)] + [zdev(j) for j in range(1, nz)]
    greet.append({"section": lax.rem(sec + 1, nsec)})
    for target in greet:
        pl.semaphore_signal(barrier, inc=1, device_id=target, device_id_type=MESH)
    pl.semaphore_wait(barrier, len(greet))

    def share(src, dst):
        return [push(src(j), dst(j), ydev(j)) for j in range(1, NY)]

    def gather_near(own, slot):
        return [push(own, slot(1), ydev(1)), push(own, slot(NY - 1), ydev(NY - 1))]

    def gather_far(copies, slot):
        on = []
        for copy, j, at in ((copies[0], 1, 0), (copies[1], NY - 1, rows // 2)):
            got([copy])
            part = pl.ds(at, rows // 2)
            on.append(push(slot(j).at[part], slot(2).at[part], ydev(j)))
        return on

    loads[0].wait()
    halo = [push(ext.at[pl.ds(rows, 32)], ext.at[pl.ds(0, 32)], seq(1))]
    loads[3].wait()
    cots = gather_near(cot, lambda j: gath.at[1, j])
    g[...] = cot[...]

    loads[1].wait()
    expand_weights(kw, 0, wbd.at[0], groups)
    loads[2].wait()
    got(halo)

    @pl.when(q == 0)
    def _():
        ext[0:32] = jnp.zeros((32, chans), BF)

    def taps_short(b):
        return jnp.concatenate(
            [ext[32 : 32 + rows, lanes(b)], ext[16 : 16 + rows, lanes(b)], ext[0:rows, lanes(b)]],
            axis=1,
        )

    def taps_long(b):
        return jnp.concatenate([mid[i, :, lanes(b)] for i in range(3)], axis=1)

    def gates(layer, taps):
        for b in range(blocks):
            pre = mm(taps(b), wbd[layer, b], NN).astype(BF).astype(F32)
            filt = jnp.tanh(pre[:, :LANE])
            gate = jax.nn.sigmoid(pre[:, LANE:])
            gated[layer, :, lanes(b)] = (filt * gate).astype(BF)
            fac[layer, 0, :, lanes(b)] = gate * (1.0 - filt * filt)
            fac[layer, 1, :, lanes(b)] = filt * gate * (1.0 - gate)

    def turn(layer):
        for b in range(blocks):
            turned = gated[layer, :, lanes(b)].T
            for i in range(per):
                d = b * per + i
                slc_s[layer, d % NY, d // NY] = turned[i * rd : (i + 1) * rd]

    def share_slices(layer):
        slc_r[layer, 0] = slc_s[layer, y]
        return share(
            lambda j: slc_s.at[layer, lax.rem(y + j, NY)], lambda j: slc_r.at[layer, j]
        )

    gates(0, taps_short)
    mid[0] = (ext[32 : 32 + rows].astype(F32) + mm(gated[0], mix[0], NN)).astype(BF)
    forth = [push(mid.at[0], mid.at[2], seq(NY)), push(mid.at[0], mid.at[1], seq(2))]

    cots = gather_far(cots, lambda j: gath.at[1, j])
    turn(0)
    slices0 = share_slices(0)
    expand_weights(kw, 1, wbd.at[1], groups)
    for copy in loads[4:]:
        copy.wait()
    got(forth)

    @pl.when(q < 2)
    def _():
        mid[1] = jnp.zeros((rows, chans), BF)

    @pl.when(q < NY)
    def _():
        mid[2] = jnp.zeros((rows, chans), BF)

    gates(1, taps_long)

    def add_loss(ref, grad):
        ref[...] = (ref[...].astype(F32) + mm(grad, head[...], TN)).astype(BF)

    dlog[0] = jnp.zeros(dlog.shape[1:], BF)

    @pl.when(last)
    def _():
        top = (mid[0].astype(F32) + mm(gated[1], mix[1], NN)).astype(BF)
        hazard = jax.nn.sigmoid(mm(head[...], top, NT))
        bins = iota(hazard.shape, 0)
        below = jnp.where(bins <= lab[...], hazard, 0.0)
        at_label = jnp.where(bins == lab[...], ev[...].astype(F32), 0.0)
        dlog[0] = (below - at_label).astype(BF)
        add_loss(g, dlog[0])

    losses = share(lambda j: dlog.at[0], lambda j: dlog.at[j])

    def cot_of_pre(layer, upstream):
        dgated = mm(upstream, mix[layer], NT)
        for b in range(blocks):
            both = jnp.concatenate(
                [
                    dgated[:, lanes(b)] * fac[layer, 0, :, lanes(b)],
                    dgated[:, lanes(b)] * fac[layer, 1, :, lanes(b)],
                ],
                axis=1,
            ).astype(BF)
            dpre[layer, :, 256 * b : 256 * (b + 1)] = both

    def back_taps(layer, b):
        return mm(dpre[layer, :, 256 * b : 256 * (b + 1)], wbd[layer, b], NT)

    cot_of_pre(1, g[...])
    for b in range(blocks):
        prods = back_taps(1, b)
        acc[:, lanes(b)] = prods[:, :LANE]
        snd_n[:, lanes(b)] = prods[:, LANE : 2 * LANE].astype(BF)
        snd_f[:, lanes(b)] = prods[:, 2 * LANE :].astype(BF)
    back = [push(snd_f, rcv_f, seq(-NY)), push(snd_n, rcv_n, seq(-2))]
    turn(1)
    slices1 = share_slices(1)

    compact = jnp.where(
        iota((768, LANE), 1) == 32 * (iota((768, LANE), 0) >> 8) + out_channel(iota((768, LANE), 0) & 255),
        1.0,
        0.0,
    ).astype(BF)
    own_group = (iota((LANE, 256), 0) >> 4) == ((iota((LANE, 256), 1) & 127) >> 4)

    def conv_terms(layer, taps):
        for b in range(blocks):
            full = mm(taps(b), dpre[layer, :, 256 * b : 256 * (b + 1)], TN)
            kept = jnp.concatenate(
                [
                    jnp.where(own_group, full[k * LANE : (k + 1) * LANE], 0.0).astype(BF)
                    for k in range(3)
                ],
                axis=1,
            )
            packed = mm(kept, compact, NN).astype(BF)
            for i in range(per):
                d = b * per + i
                cnv_s[layer, d % NY, d // NY] = packed[i * rd : (i + 1) * rd]
        return share(
            lambda j: cnv_s.at[layer, lax.rem(y + j, NY)], lambda j: cnv_r.at[layer, j - 1]
        )

    convs1 = conv_terms(1, taps_long)

    def quarter(layer, lo, w):
        left = jnp.concatenate(
            [slc_r[layer, j].reshape(nz * rd, rows) for j in range(NY)], axis=1
        )
        right = gath[layer, :, :, lo : lo + w].reshape(NY * rows, w)
        return mm(left, right, NN).reshape(nz, rd, w)

    def spread(buf, dst):
        return [
            push(buf.at[lax.rem(z + j, nz)], dst.at[j - 1], zdev(j)) for j in range(1, nz)
        ]

    got(slices1)
    got(cots)
    got(losses)
    for copy in cots:
        copy.wait_send()

    @pl.when(last)
    def _():
        for j in range(1, NY):
            add_loss(gath.at[1, j], dlog[j])

    def ring(own, done):
        right_s, right_r, left_s, left_r = ring_bufs
        arrived, at = None, 0
        for t in range(1, nz // 2 + 1):
            dist = nz // 2 - t + 1
            to_r, to_l = lax.rem(z + dist, nz), lax.rem(z - dist + nz, nz)
            size = 1 if t == 1 else 2
            if arrived is not None:
                was, copies = arrived
                got(copies)
            for d in range(2):
                if t > 1 or d == 0:
                    v = own(to_r, d)
                    if t > 2 or (t == 2 and d == 0):
                        v = v + right_r[was + d].astype(F32)
                    right_s[at + d] = v.astype(BF)
                if t > 1 or d == 1:
                    v = own(to_l, d)
                    if t > 2 or (t == 2 and d == 1):
                        v = v + left_r[was + (0 if t == 2 else d)].astype(F32)
                    left_s[at + (0 if t == 1 else d)] = v.astype(BF)
            copies = [
                push(right_s.at[pl.ds(at, size)], right_r.at[pl.ds(at, size)], zdev(1)),
                push(left_s.at[pl.ds(at, size)], left_r.at[pl.ds(at, size)], zdev(nz - 1)),
            ]
            arrived = (at, copies)
            at += size
            yield
        was, copies = arrived
        got(copies)
        for d in range(2):
            v = own(z, d)
            if nz > 2:
                v = v + right_r[was + d].astype(F32) + left_r[was + d].astype(F32)
            elif d == 0:
                v = v + right_r[was].astype(F32)
            else:
                v = v + left_r[was].astype(F32)
            done(d, v)
        yield

    half = rd // 2
    for lo in range(0, chans, 256):
        zown[1, :, :, lo : lo + 256] = quarter(1, lo, 256)

    def conv_sum(layer, copies):
        got(copies)
        sums = cnv_s[layer, y].astype(F32)
        for j in range(NY - 1):
            sums = sums + cnv_r[layer, j].astype(F32)
        zown[layer, :, :, chans : chans + LANE] = sums
        return sums

    def put_conv(layer, lo, sums):
        for k in range(3):
            cg_buf[0, layer, k, lo // 16 : (lo + sums.shape[0]) // 16] = sums[
                :, 32 * k : 32 * (k + 1)
            ].reshape(sums.shape[0] // 16, 16, 32)

    def finish1(d, v):
        mg_buf[0, d * half : (d + 1) * half, 1, :] = v[:, 0:chans]
        put_conv(1, d * half, v[:, chans:])

    conv_sum(1, convs1)
    ring1 = ring(lambda e, d: zown[1, e, d * half : (d + 1) * half, :], finish1)
    next(ring1, None)

    got(back)

    @pl.when(q >= nq - 2)
    def _():
        rcv_n[...] = jnp.zeros((rows, chans), BF)

    @pl.when(q >= nq - NY)
    def _():
        rcv_f[...] = jnp.zeros((rows, chans), BF)

    btw[...] = (
        g[...].astype(F32) + acc[...] + rcv_n[...].astype(F32) + rcv_f[...].astype(F32)
    ).astype(BF)
    def lane_slot(lo, w):
        return lambda j: gath.at[0, j, :, pl.ds(lo, w)]

    slots = [lane_slot(lo, w) for lo, w, _ in chunks]
    shared = [gather_near(slot(0), slot) for slot in slots]
    next(ring1, None)
    cot_of_pre(0, btw[...])
    for b in range(blocks):
        prods = back_taps(0, b)
        acc[:, lanes(b)] = prods[:, :LANE]
        tap1[0:rows, lanes(b)] = prods[:, LANE : 2 * LANE]
        tap2[0:rows, lanes(b)] = prods[:, 2 * LANE :]
    hal_s[0:16] = tap2[0:16].astype(BF)
    hal_s[16:32] = (tap1[0:16] + tap2[16:32]).astype(BF)
    back_halo = push(hal_s, hal_r, seq(-1))
    shared[0] = gather_far(shared[0], slots[0])
    convs0 = conv_terms(0, taps_short)
    shared[1] = gather_far(shared[1], slots[1])
    next(ring1, None)
    tap1[rows : rows + 16] = jnp.zeros((16, chans), F32)
    tap2[rows : rows + 32] = jnp.zeros((32, chans), F32)
    for c in range(2, len(chunks)):
        shared[c] = gather_far(shared[c], slots[c])
    got(slices0)
    over0 = []

    def cross(c):
        lo, w, conv = chunks[c]
        got(shared[c])
        block = quarter(0, lo, w)
        zown[0, :, :, lo : lo + w] = block
        zs0[c][:, :, 0:w] = block.astype(BF)
        if conv:
            zs0[c][:, :, w : w + LANE] = conv_sum(0, convs0).astype(BF)
        over0.append(spread(zs0[c], zr0[c]))
        if c == 0:
            next(ring1, None)

    cross(0)
    back_halo.wait_recv()

    @pl.when(q == nq - 1)
    def _():
        hal_r[...] = jnp.zeros((32, chans), BF)

    total = btw[...].astype(F32) + acc[...] + tap1[16 : 16 + rows] + tap2[32 : 32 + rows]
    ig_buf[0, 0 : rows - 32] = total[0 : rows - 32].astype(BF)
    ig_buf[0, rows - 32 : rows] = (total[rows - 32 :] + hal_r[...].astype(F32)).astype(BF)
    def write(i, src, dst):
        copy = pltpu.make_async_copy(src, dst, osem.at[i])
        copy.start()
        return copy

    writes = [write(0, ig_buf, ig_out)]
    to_prev = push(ig_buf.at[0], nxt, {"section": lax.rem(sec + nsec - 1, nsec)})

    for c in range(1, len(chunks)):
        cross(c)
    for _ in range(nz // 2 - 3):
        next(ring1, None)

    def total_of(own, bufs, lo, w):
        v = own
        for j in range(nz - 1):
            v = v + bufs[j, :, lo : lo + w].astype(F32)
        return v

    to_prev.wait_recv()

    @pl.when(last)
    def _():
        nc_buf[0] = g[...]

    @pl.when(jnp.logical_not(last))
    def _():
        nc_buf[0] = nxt[...]

    writes.append(write(1, nc_buf, nc_out))

    for c, (lo, w, conv) in enumerate(chunks):
        got(over0[c])
        mg_buf[0, :, 0, lo : lo + w] = total_of(zown[0, z, :, lo : lo + w], zr0[c], 0, w)
        if conv:
            put_conv(0, 0, total_of(zown[0, z, :, chans : chans + LANE], zr0[c], w, LANE))

    writes += [write(2, mg_buf, mg_out), write(3, cg_buf, cg_out)]
    for copy in writes:
        copy.wait()
    for copy in sends:
        if all(copy is not c for c in cots):
            copy.wait_send()


def hand_over(*refs):
    srcs, dsts, bufs, (sem_in, sem_out) = refs[:4], refs[4:8], refs[8:12], refs[12:]
    fetch = [pltpu.make_async_copy(a, b, sem_in.at[i]) for i, (a, b) in enumerate(zip(srcs, bufs))]
    store = [pltpu.make_async_copy(a, b, sem_out.at[i]) for i, (a, b) in enumerate(zip(bufs, dsts))]
    for copy in fetch:
        copy.start()
    for before, after in zip(fetch, store):
        before.wait()
        after.start()
    for copy in store:
        copy.wait()


def solution(mesh):
    nsec, nq = mesh.shape["section"], mesh.shape["seq"]
    nz = nq // NY

    def body(x, cot, kernel_weight, blend, head, labels, events):
        _, rows, chans = x.shape
        groups, gin, gout = kernel_weight.shape[3:]
        rd = chans // nq
        blocks = chans // LANE
        kw = jnp.transpose(kernel_weight[0], (0, 1, 3, 4, 2)).reshape(6, gin * gout, groups)
        any_ = pl.BlockSpec(memory_space=pl.ANY)
        vm = pl.BlockSpec(memory_space=pltpu.VMEM)
        act = pltpu.VMEM((rows, chans), BF)
        quarter = chans // 4
        chunks = [(0, 2 * quarter, False), (2 * quarter, quarter, False), (3 * quarter, quarter, True)]
        wide = [w + (LANE if conv else 0) for _, w, conv in chunks]
        n_push = 1 + 4 + 2 + 6 + 3 + 2 + 6 + nz + 16 + 2 + 4 * (nz - 1)
        bins = head.shape[1]
        scratch = [
            pltpu.VMEM((rows + 32, chans), BF),
            act,
            pltpu.VMEM((6, gin * gout, groups), BF),
            pltpu.VMEM((2, chans, chans), BF),
            pltpu.VMEM((bins, chans), BF),
            pltpu.VMEM((1, rows), jnp.int32),
            pltpu.VMEM((1, rows), jnp.int32),
            pltpu.VMEM((2, blocks, 3 * LANE, 2 * LANE), BF),
            pltpu.VMEM((2, rows, chans), BF),
            pltpu.VMEM((2, 2, rows, chans), F32),
            pltpu.VMEM((3, rows, chans), BF),
            pltpu.VMEM((2, rows, 2 * chans), BF),
            pltpu.VMEM((rows, chans), F32),
            act,
            act,
            act,
            act,
            pltpu.VMEM((rows + 16, chans), F32),
            pltpu.VMEM((rows + 32, chans), F32),
            pltpu.VMEM((32, chans), BF),
            pltpu.VMEM((32, chans), BF),
            act,
            pltpu.VMEM((2, NY, rows, chans), BF),
            pltpu.VMEM((2, NY, nz, rd, rows), BF),
            pltpu.VMEM((2, NY, nz, rd, rows), BF),
            pltpu.VMEM((NY, bins, rows), BF),
            pltpu.VMEM((2, NY, nz, rd, LANE), BF),
            pltpu.VMEM((2, NY - 1, nz, rd, LANE), BF),
            pltpu.VMEM((2, nz, rd, chans + LANE), F32),
            pltpu.SemaphoreType.DMA((8,)),
            pltpu.SemaphoreType.DMA((n_push,)),
            pltpu.SemaphoreType.DMA((n_push,)),
        ]
        shapes = (
            jax.ShapeDtypeStruct((1, rows, chans), BF),
            jax.ShapeDtypeStruct((1, rows, chans), BF),
            jax.ShapeDtypeStruct((1, rd, 2, chans), F32),
            jax.ShapeDtypeStruct((1, 2, 3, groups // nq, gin, gout), F32),
        )
        scratch += [pltpu.VMEM(o.shape, o.dtype) for o in shapes] + [pltpu.SemaphoreType.DMA((4,))]
        scratch += [pltpu.VMEM((nz, rd, w), BF) for w in wide]
        scratch += [pltpu.VMEM((nz - 1, rd, w), BF) for w in wide]
        scratch += [pltpu.VMEM((nz - 1, rd // 2, chans + LANE), BF)] * 4
        outs = pl.pallas_call(
            functools.partial(kernel, nz, nsec, chunks),
            out_shape=shapes,
            in_specs=[any_] * 7,
            out_specs=(any_,) * 4,
            scratch_shapes=scratch,
            compiler_params=pltpu.CompilerParams(
                collective_id=0, has_side_effects=True, vmem_limit_bytes=58 * 1024 * 1024
            ),
        )(x, cot, kw, blend, head.T, labels.reshape(1, rows), events.reshape(1, rows))
        return pl.pallas_call(
            hand_over,
            out_shape=shapes,
            in_specs=[any_] * 4,
            out_specs=(any_,) * 4,
            scratch_shapes=[pltpu.VMEM(o.shape, o.dtype) for o in shapes]
            + [pltpu.SemaphoreType.DMA((4,))] * 2,
        )(*outs)

    return jax.shard_map(
        body,
        mesh=mesh,
        in_specs=(
            P("section", "seq", None),
            P("section", "seq", None),
            P("section", None, None, None, None, None),
            P("section", None, None, None),
            P(),
            P("seq"),
            P("seq"),
        ),
        out_specs=(
            P("section", "seq", None),
            P("section", "seq", None),
            P("section", "seq", None, None),
            P("section", None, None, "seq", None, None),
        ),
        check_vma=False,
    )
```
